32 devices in a mesh: wide: 8 (over z, x), narrow: 4 (over y, core).
Axes of the slice: x: 2, y: 2, z: 4, core: 2. Of those that a mesh axis runs over, the one named last changes fastest.
Arguments:
- right_side: float32 [4, 128, 12, 128], P('narrow', 'wide'), may hold values from -160 to 160
- hop_blocks: bfloat16 [4, 128, 9, 64, 128], P('narrow', 'wide'), may hold values from -2 to 6
- restriction: float32 [4, 128, 64, 128], P('narrow', 'wide'), may hold values from -0.25 to 0.25
Outputs:
- solution_field: float32 [4, 128, 12, 128], P('narrow', 'wide')
- coarse_residual: float32 [4, 32, 12, 128], P(None, 'wide')
The draws below stay inside these ranges and needn't reach their ends.
All inputs are finite; a program needn't handle non-finite values.
Results may differ from the reference program's by a relative error of at most 0.0053.
Values may be sent and summed in bfloat16 or wider, within the bound.
No kernel may reach another device: no remote copies, remote signals or barrier semaphores. Data moves between devices by JAX's collectives and lax.ppermute only.
A program may use at most 64 MiB of HBM per device.

```python
import math
import jax
import jax.numpy as jnp
from jax import lax

DOF = 64
DOF3 = 64
RHS = 12
ITERS = 4
LX = 8
YLOC = 2
LY = 16
LZ = 1
NT = 4
XYZ = 128
XYZ3 = 32


def draw_right_side(key, part):
    shape = (NT, XYZ, RHS, 2 * DOF)
    key_base, key_cols, key_rough, key_blocks = jax.random.split(key, 4)
    time_pos = lax.broadcasted_iota(jnp.float32, shape, 0) / NT
    site_pos = lax.broadcasted_iota(jnp.float32, shape, 1) / XYZ
    ramp = jnp.exp(math.log(3.0) * (time_pos + site_pos))
    columns = jnp.exp(jax.random.uniform(key_cols, (1, 1, RHS, 1), jnp.float32, 0.0, math.log(10.0)))
    block_count = XYZ // (LX * YLOC)
    owner = jnp.arange(XYZ, dtype=jnp.int32) // (LX * YLOC)
    block_scale = jnp.exp(jax.random.uniform(key_blocks, (NT, block_count, RHS), jnp.float32, -0.5 * math.log(3.0), 0.5 * math.log(3.0)))
    spread = jnp.take(block_scale, owner, axis=1)[..., None]
    rough = jax.random.uniform(key_rough, shape, jnp.float32, 0.5, 1.5)
    base = jnp.clip(jax.random.normal(key_base, shape, jnp.float32), -4.0, 4.0)
    return ramp * columns * spread * rough * base / 6.0


def draw_hop_blocks(key, part):
    shape = (NT, XYZ, 9, DOF, 2 * DOF)
    key_noise, key_diag, key_imag, key_level, key_scale, key_strength = jax.random.split(key, 6)
    sigma = 0.35 / math.sqrt(2.0 * DOF)
    block_count = XYZ // (LX * YLOC)
    owner = jnp.arange(XYZ, dtype=jnp.int32) // (LX * YLOC)
    draw_scale = jnp.exp(jax.random.uniform(key_scale, (), jnp.float32, math.log(0.8), math.log(1.25)))
    draw_strength = jnp.exp(jax.random.uniform(key_strength, (), jnp.float32, math.log(0.7), math.log(1.4)))
    diag_table = jnp.exp(jax.random.uniform(key_diag, (NT, block_count), jnp.float32, math.log(1.5), math.log(4.0)))
    imag_table = jax.random.uniform(key_imag, (NT, block_count), jnp.float32, -1.5, 1.5)
    level_table = jnp.exp(jax.random.uniform(key_level, (NT, block_count), jnp.float32, -0.5 * math.log(3.0), 0.5 * math.log(3.0)))
    diag_real = jnp.take(draw_scale * diag_table, owner, axis=1)[:, :, None, None, None]
    diag_imag = jnp.take(imag_table, owner, axis=1)[:, :, None, None, None]
    level = jnp.take(draw_strength * level_table, owner, axis=1)[:, :, None, None, None]
    noise = jnp.clip(jax.random.normal(key_noise, shape, jnp.float32) * sigma, -4.0 * sigma, 4.0 * sigma)
    direction = lax.broadcasted_iota(jnp.int32, shape, 2)
    row_index = lax.broadcasted_iota(jnp.int32, shape, 3)
    col_index = lax.broadcasted_iota(jnp.int32, shape, 4)
    real_diag = jnp.where((direction == 0) & (row_index == col_index), diag_real, 0.0)
    imag_diag = jnp.where((direction == 0) & (col_index == row_index + DOF), diag_imag, 0.0)
    return (noise * level + real_diag + imag_diag).astype(jnp.bfloat16)


def shard_levels(key, dims, shards, least, largest):
    gain = 1.0
    for axis_at, shards_of in shards:
        heights = jax.random.uniform(jax.random.fold_in(jax.random.fold_in(key, 6), axis_at), (shards_of,), jnp.float32, least / len(shards), largest / len(shards))
        gain = gain * jnp.repeat(jnp.exp(heights), dims[axis_at] // shards_of).reshape((-1,) + (1,) * (len(dims) - 1 - axis_at))
    return gain


def centred(rng, dims, deviation, bound, cuts=(), kind=jnp.bfloat16):
    array = jax.random.normal(rng, dims, jnp.float32) * deviation
    if len(cuts) > 0:
        array = shard_levels(rng, dims, cuts, -0.22, 0.18) * array
    return jnp.clip(array, min=-bound, max=bound).astype(kind)


def setup_inputs(seed: int = 0) -> dict:
    keys = jax.random.split(jax.random.key(seed), 4)
    right_side = draw_right_side(jax.random.fold_in(keys[3], 71), 0)
    hop_blocks = draw_hop_blocks(jax.random.fold_in(keys[3], 71), 0)
    restriction = centred(keys[2], (NT, XYZ, DOF3, 2 * DOF), (8 * DOF) ** -0.5, 0.25, ((0, 4), (1, 8)), jnp.float32)
    return {"right_side": right_side, "hop_blocks": hop_blocks, "restriction": restriction}


def complex_pair(vector):
    half = vector.shape[-1] // 2
    real_part = vector[..., :half]
    imag_part = vector[..., half:]
    first = jnp.concatenate([real_part, -imag_part], -1)
    second = jnp.concatenate([imag_part, real_part], -1)
    return first, second


def spatial_views(slab):
    lattice = slab.reshape(LZ, LY, LX, slab.shape[1], slab.shape[2])
    views = [lattice,
             jnp.roll(lattice, -1, 2), jnp.roll(lattice, 1, 2),
             jnp.roll(lattice, -1, 1), jnp.roll(lattice, 1, 1),
             jnp.roll(lattice, -1, 0), jnp.roll(lattice, 1, 0)]
    return [view.reshape(slab.shape) for view in views]


def operate(rounded, hop_blocks):
    def one_slice(tindex):
        here = lax.dynamic_index_in_dim(rounded, tindex, 0, keepdims=False)
        later = lax.dynamic_index_in_dim(rounded, (tindex + 1) % NT, 0, keepdims=False)
        earlier = lax.dynamic_index_in_dim(rounded, (tindex + NT - 1) % NT, 0, keepdims=False)
        blocks = lax.dynamic_index_in_dim(hop_blocks, tindex, 0, keepdims=False)
        views = spatial_views(here) + [later, earlier]
        total = jnp.zeros((here.shape[0], here.shape[1], DOF * 2), jnp.float32)
        for direction in range(9):
            first, second = complex_pair(views[direction])
            block = blocks[:, direction].astype(jnp.float32)
            out_re = jnp.einsum("sak,srk->sra", block, first.astype(jnp.float32))
            out_im = jnp.einsum("sak,srk->sra", block, second.astype(jnp.float32))
            total = total + jnp.concatenate([out_re, out_im], -1)
        return total
    return lax.map(one_slice, jnp.arange(NT, dtype=jnp.int32))


def cmul(alpha_re, alpha_im, vector):
    half = vector.shape[-1] // 2
    real_part = vector[..., :half]
    imag_part = vector[..., half:]
    are = alpha_re[:, None]
    aim = alpha_im[:, None]
    return jnp.concatenate([are * real_part - aim * imag_part, are * imag_part + aim * real_part], -1)


def reference(right_side, hop_blocks, restriction):
    solution_field = jnp.zeros_like(right_side)
    residual = right_side
    half = DOF
    for step in range(ITERS):
        rounded = residual.astype(jnp.bfloat16)
        image = operate(rounded, hop_blocks)
        inner_re = jnp.sum(image * residual, axis=(0, 1, 3))
        inner_im = jnp.sum(image[..., :half] * residual[..., half:] - image[..., half:] * residual[..., :half], axis=(0, 1, 3))
        power = jnp.sum(image * image, axis=(0, 1, 3))
        alpha_re = inner_re / power
        alpha_im = inner_im / power
        solution_field = solution_field + cmul(alpha_re, alpha_im, residual)
        residual = residual - cmul(alpha_re, alpha_im, image)
    first, second = complex_pair(residual)
    out_re = jnp.einsum("tsak,tsrk->tsra", restriction, first, precision=lax.Precision.HIGHEST)
    out_im = jnp.einsum("tsak,tsrk->tsra", restriction, second, precision=lax.Precision.HIGHEST)
    persite = jnp.concatenate([out_re, out_im], -1)
    grouped = persite.reshape(NT, LZ, LY // 2, 2, LX // 2, 2, RHS, 2 * DOF3)
    coarse_residual = jnp.sum(grouped, axis=(3, 5)).reshape(NT, XYZ3, RHS, 2 * DOF3)
    return solution_field, coarse_residual
```

```python
import functools

import jax
import jax.numpy as jnp
from jax import lax
from jax.experimental import pallas as pl
from jax.experimental.pallas import tpu as pltpu
from jax.sharding import PartitionSpec as P

ITERS = 4
YLOC = 2
LY = 16
STEP_SCALE = 0.25
SLOT = 32
VMEM_LIMIT = 24 * 1024 * 1024


def tile_starts(rhs):
    starts = list(range(0, rhs - 7, 8))
    if rhs % 8:
        starts.append(rhs - 8)
    return starts


def load_site(ref, site, sites, rhs, by_rhs):
    tiles = []
    for start in tile_starts(rhs):
        if by_rhs:
            tiles.append(ref[pl.ds(start * sites + site, 8, stride=sites), :])
        else:
            tiles.append(ref[site * rhs + start : site * rhs + start + 8, :])
    return jnp.concatenate(tiles, 0)


def store_site(ref, site, sites, rhs, value, by_rhs):
    for at, start in enumerate(tile_starts(rhs)):
        tile = value[8 * at : 8 * at + 8]
        if by_rhs:
            ref[pl.ds(start * sites + site, 8, stride=sites), :] = tile
        else:
            ref[site * rhs + start : site * rhs + start + 8, :] = tile


def operand(block, sign):
    first = block * sign
    second = pltpu.roll(block, block.shape[-1] // 2, 1)
    highs = []
    lows = []
    for part in (first, second):
        high = part.astype(jnp.bfloat16)
        highs.append(high)
        lows.append((part - high.astype(jnp.float32)).astype(jnp.bfloat16))
    return jnp.concatenate(highs + lows, 0)


def lane_sign(width):
    lane = lax.broadcasted_iota(jnp.int32, (1, width), 1)
    return jnp.where(lane < width // 2, 1.0, -1.0).astype(jnp.float32)


def prepare(field_ref, table_ref, first_slot, sites, rhs, by_rhs):
    sign = lane_sign(field_ref.shape[-1])
    for site in range(sites):
        block = load_site(field_ref, site, sites, rhs, by_rhs)
        table_ref[first_slot + site] = operand(block, sign)


def site_product(slots, blocks):
    rows = slots[0].shape[0] // 4
    left = jnp.concatenate(slots, -1)
    right = jnp.concatenate(blocks, -1)
    total = lax.dot_general(
        left, right, (((1,), (1,)), ((), ())), preferred_element_type=jnp.float32
    )
    real_part = total[0:rows] + total[2 * rows : 3 * rows]
    imag_part = total[rows : 2 * rows] + total[3 * rows : 4 * rows]
    return jnp.concatenate([real_part, imag_part], -1) * STEP_SCALE


def columns_of(total, lanes, slot):
    summed = jnp.sum(total, axis=-1, keepdims=True)
    return jnp.where(lanes == slot, summed, 0.0)


def pair_slots(power):
    slots = []
    at = sum(2 * earlier + 1 for earlier in range(1, power))
    for other in range(power):
        slots.append((other, at, at + 1))
        at += 2
    slots.append((power, at, None))
    return slots


def gram_columns(power, refs, period):
    width = refs[0].shape[-1]
    rows = refs[0].shape[0]
    lanes = lax.broadcasted_iota(jnp.int32, (period, width), 1)
    sign = lane_sign(width)
    out = jnp.zeros((period, width), jnp.float32)
    for other, real_lane, imag_lane in pair_slots(power):
        real_sum = None
        imag_sum = None
        for base in range(0, rows, period):
            mine = refs[power][base : base + period, :]
            theirs = refs[other][base : base + period, :]
            real_term = mine * theirs
            real_sum = real_term if real_sum is None else real_sum + real_term
            if imag_lane is not None:
                turned = pltpu.roll(theirs, width // 2, 1)
                imag_term = mine * turned
                imag_sum = imag_term if imag_sum is None else imag_sum + imag_term
        out = out + columns_of(real_sum, lanes, real_lane)
        if imag_lane is not None:
            out = out + columns_of(imag_sum * sign, lanes, imag_lane)
    return out


def near_kernel(power, depth, rhs, wrap_z, *refs):
    fields = refs[: power + 1]
    hops = refs[power + 1]
    near_ref = refs[power + 2]
    table = refs[-1]
    sites = hops.shape[0]
    extent = sites // depth
    prepare(fields[power], table, 0, sites, rhs, power == 0)
    for site in range(sites):
        y, x = divmod(site, extent)
        chosen = [(0, site), (1, y * extent + (x + 1) % extent), (2, y * extent + (x - 1) % extent)]
        if y + 1 < depth:
            chosen.append((3, site + extent))
        if y > 0:
            chosen.append((4, site - extent))
        if wrap_z:
            chosen += [(5, site), (6, site)]
        value = site_product([table[at] for _, at in chosen], [hops[site, d] for d, _ in chosen])
        store_site(near_ref, site, sites, rhs, value, False)
    if power > 0:
        gram_ref = refs[power + 3]
        gram_ref[...] = gram_columns(power, fields, gram_ref.shape[0])
    else:
        start_ref = refs[3]
        for site in range(sites):
            block = load_site(fields[0], site, sites, rhs, True)
            store_site(start_ref, site, sites, rhs, block, False)


def far_kernel(depth, rhs, wrap_z, by_rhs, *refs):
    near_ref, hops, fwd_ref, back_ref, later_ref, earlier_ref = refs[:6]
    out_ref, table = refs[-2:]
    sites = hops.shape[0]
    extent = sites // depth
    ahead = 2 * sites
    behind = ahead + extent
    above = behind + extent
    below = above + sites
    prepare(later_ref, table, 0, sites, rhs, by_rhs)
    prepare(earlier_ref, table, sites, sites, rhs, by_rhs)
    prepare(fwd_ref, table, ahead, extent, rhs, by_rhs)
    prepare(back_ref, table, behind, extent, rhs, by_rhs)
    if not wrap_z:
        prepare(refs[6], table, above, sites, rhs, by_rhs)
        prepare(refs[7], table, below, sites, rhs, by_rhs)
    for site in range(sites):
        y, x = divmod(site, extent)
        chosen = [(7, site), (8, sites + site)]
        if y + 1 == depth:
            chosen.append((3, ahead + x))
        if y == 0:
            chosen.append((4, behind + x))
        if not wrap_z:
            chosen += [(5, above + site), (6, below + site)]
        value = site_product([table[at] for _, at in chosen], [hops[site, d] for d, _ in chosen])
        value = value + load_site(near_ref, site, sites, rhs, False)
        store_site(out_ref, site, sites, rhs, value, False)


def pack_kernel(rhs, *refs):
    fields = refs[: ITERS + 1]
    grams = refs[ITERS + 1 : -1]
    out_ref = refs[-1]
    period, width = grams[0].shape
    total = gram_columns(ITERS, fields, period)
    for gram in grams:
        total = total + gram[...]
    folded = total
    for turn in range(1, period // rhs):
        folded = folded + pltpu.roll(total, turn * rhs, 0)
    per_row = width // SLOT
    row = lax.broadcasted_iota(jnp.int32, (period, width), 0)
    spread = jnp.zeros((period, width), jnp.float32)
    for m in range(per_row):
        part = jnp.where(row % per_row == m, folded, 0.0)
        spread = spread + (pltpu.roll(part, SLOT * m, 1) if m else part)
    for q in range(-(-rhs // per_row)):
        summed = spread[q * per_row : q * per_row + 1]
        for m in range(1, min(per_row, rhs - q * per_row)):
            summed = summed + spread[q * per_row + m : q * per_row + m + 1]
        out_ref[q : q + 1, :] = summed


def cmulc(a, b):
    return (a[0] * b[0] + a[1] * b[1], a[0] * b[1] - a[1] * b[0])


def cmul(a, b):
    return (a[0] * b[0] - a[1] * b[1], a[0] * b[1] + a[1] * b[0])


def cadd(a, b):
    return (a[0] + b[0], a[1] + b[1])


def csub(a, b):
    return (a[0] - b[0], a[1] - b[1])


def final_kernel(depth, rhs, *refs):
    fields = refs[: ITERS + 1]
    packed, restriction = refs[ITERS + 1 : ITERS + 3]
    sol_ref, coarse_ref, res_ref, kept_ref = refs[ITERS + 3 :]
    width = fields[0].shape[-1]
    total_rows = fields[0].shape[0]
    period = rhs
    while period % 8:
        period *= 2
    per_row = width // SLOT
    row = lax.broadcasted_iota(jnp.int32, (period, width), 0) % rhs
    summed = packed[...]
    gram = jnp.zeros((period, width), jnp.float32)
    for r in range(rhs):
        q, m = divmod(r, per_row)
        line = jnp.broadcast_to(summed[q : q + 1], (period, width))
        if m:
            line = pltpu.roll(line, width - SLOT * m, 1)
        gram = jnp.where(row == r, line, gram)

    def column(lane):
        return gram[:, lane : lane + 1]

    def zero():
        return jnp.zeros((period, 1), jnp.float32)

    products = [[None] * (ITERS + 1) for _ in range(ITERS + 1)]
    for power in range(1, ITERS + 1):
        for other, real_lane, imag_lane in pair_slots(power):
            re = column(real_lane)
            im = column(imag_lane) if imag_lane is not None else None
            products[power][other] = (re, im)
            if other and imag_lane is not None:
                products[other][power] = (re, -im)

    def times(entry, value):
        if entry[1] is None:
            return (entry[0] * value[0], entry[0] * value[1])
        return cmul(entry, value)

    coeffs = [(jnp.ones((period, 1), jnp.float32), zero())]
    solution = []
    overlaps = [products[i][0] for i in range(1, ITERS + 1)]
    for step in range(ITERS):
        inner = None
        for i in range(step + 1):
            term = cmulc(coeffs[i], overlaps[i])
            inner = term if inner is None else cadd(inner, term)
        images = []
        for i in range(ITERS):
            value = None
            for j in range(step + 1):
                term = times(products[i + 1][j + 1], coeffs[j])
                value = term if value is None else cadd(value, term)
            images.append(value)
        power = None
        for i in range(step + 1):
            term = coeffs[i][0] * images[i][0] + coeffs[i][1] * images[i][1]
            power = term if power is None else power + term
        alpha = (inner[0] / power, inner[1] / power)
        overlaps = [csub(o, cmul(alpha, im)) for o, im in zip(overlaps, images)]
        scaled = [cmul(alpha, c) for c in coeffs]
        for i, value in enumerate(scaled):
            if i < len(solution):
                solution[i] = cadd(solution[i], value)
            else:
                solution.append(value)
        grown = []
        for i in range(step + 2):
            if i == 0:
                grown.append(coeffs[0])
            elif i <= step:
                grown.append(csub(coeffs[i], scaled[i - 1]))
            else:
                grown.append((-scaled[i - 1][0], -scaled[i - 1][1]))
        coeffs = grown
    sign = lane_sign(width)

    def spread(value, factor):
        real_part = jnp.broadcast_to(value[0] * factor, (period, width))
        imag_part = jnp.broadcast_to(value[1] * factor, (period, width)) * (-sign)
        return real_part, imag_part

    res_co = [spread(c, 1.0) for c in coeffs]
    sol_co = [spread(c, STEP_SCALE) for c in solution]
    for base in range(0, total_rows, period):
        res = None
        sol = None
        for i in range(ITERS + 1):
            value = fields[i][base : base + period, :]
            turned = pltpu.roll(value, width // 2, 1)
            if i == 0:
                res = value
            else:
                res = res + res_co[i][0] * value + res_co[i][1] * turned
            if i < ITERS:
                term = sol_co[i][0] * value + sol_co[i][1] * turned
                sol = term if sol is None else sol + term
        kept_ref[base : base + period, :] = sol
        res_ref[base : base + period, :] = res
    sites = restriction.shape[0]
    extent = sites // depth
    cells = extent // 2
    for cell in range(cells):
        lefts = []
        rights = []
        for y in range(depth):
            for site in (y * extent + 2 * cell, y * extent + 2 * cell + 1):
                block = load_site(res_ref, site, sites, rhs, False)
                turned = pltpu.roll(block, width // 2, 1)
                lefts.append(jnp.concatenate([block * sign, turned], 0))
                rights.append(restriction[site])
        total = lax.dot_general(
            jnp.concatenate(lefts, -1),
            jnp.concatenate(rights, -1),
            (((1,), (1,)), ((), ())),
            precision=lax.Precision.HIGHEST,
            preferred_element_type=jnp.float32,
        )
        half = total.shape[0] // 2
        value = jnp.concatenate([total[:half], total[half:]], -1)
        store_site(coarse_ref, cell, cells, rhs, value, True)
    for site in range(sites):
        store_site(sol_ref, site, sites, rhs, load_site(kept_ref, site, sites, rhs, False), True)


def vmem(count):
    return [pl.BlockSpec(memory_space=pltpu.VMEM)] * count


def call(kernel, outs, *args, scratch=(), name=None):
    single = not isinstance(outs, (list, tuple))
    return pl.pallas_call(
        kernel,
        out_shape=outs,
        in_specs=vmem(len(args)),
        out_specs=pl.BlockSpec(memory_space=pltpu.VMEM) if single else tuple(vmem(len(outs))),
        scratch_shapes=list(scratch),
        compiler_params=pltpu.CompilerParams(vmem_limit_bytes=VMEM_LIMIT),
        name=name,
    )(*args)


def per_device(right_side, hop_blocks, restriction):
    sites, rhs, width = right_side.shape[1:]
    extent = sites // YLOC
    rows_y = LY // YLOC
    wide = lax.axis_size("wide")
    narrow = lax.axis_size("narrow")
    wrap_z = wide <= rows_y
    period = rhs
    while period % 8:
        period *= 2
    tile_rows = 8 * len(tile_starts(rhs))
    total_rows = sites * rhs
    half = extent * rhs
    f32 = jnp.float32
    field_shape = jax.ShapeDtypeStruct((total_rows, width), f32)
    gram_shape = jax.ShapeDtypeStruct((period, width), f32)
    hops = hop_blocks[0]

    up_y = [(i, i // rows_y * rows_y + (i + 1) % rows_y) for i in range(wide)]
    down_y = [(b, a) for a, b in up_y]
    up_z = [(i, (i + rows_y) % wide) for i in range(wide)]
    down_z = [(b, a) for a, b in up_z]
    up_t = [(i, (i + 1) % narrow) for i in range(narrow)]
    down_t = [(b, a) for a, b in up_t]

    by_rhs = jnp.transpose(right_side[0], (1, 0, 2))
    field = by_rhs.reshape(total_rows, width)
    first_row = by_rhs[:, :extent].reshape(half, width)
    last_row = by_rhs[:, sites - extent :].reshape(half, width)
    fields = []
    grams = []
    for power in range(ITERS):
        if power:
            field = fields[power]
            first_row = field[:half]
            last_row = field[total_rows - half :]
        fwd = lax.ppermute(first_row, "wide", down_y)
        back = lax.ppermute(last_row, "wide", up_y)
        later = lax.ppermute(field, "narrow", down_t)
        earlier = lax.ppermute(field, "narrow", up_t)
        received = [fwd, back, later, earlier]
        if not wrap_z:
            received += [lax.ppermute(field, "wide", down_z), lax.ppermute(field, "wide", up_z)]
        near, other = call(
            functools.partial(near_kernel, power, YLOC, rhs, wrap_z),
            [field_shape, gram_shape if power else field_shape],
            *(fields if power else [field]),
            hops,
            scratch=[pltpu.VMEM((sites, 4 * tile_rows, width), jnp.bfloat16)],
            name=f"near{power}",
        )
        if power:
            grams.append(other)
        else:
            fields.append(other)
        slots = 2 * sites + 2 * extent + (0 if wrap_z else 2 * sites)
        fields.append(
            call(
                functools.partial(far_kernel, YLOC, rhs, wrap_z, power == 0),
                field_shape,
                near,
                hops,
                *received,
                scratch=[pltpu.VMEM((slots, 4 * tile_rows, width), jnp.bfloat16)],
                name=f"far{power}",
            )
        )
    per_row = width // SLOT
    packed_rows = -(-rhs // per_row)
    packed = call(
        functools.partial(pack_kernel, rhs),
        jax.ShapeDtypeStruct((packed_rows, width), f32),
        *fields,
        *grams,
        name="pack",
    )
    copies = jnp.broadcast_to(packed[None], (wide * narrow, packed_rows, width))
    swapped = lax.all_to_all(copies, ("wide", "narrow"), 0, 0)
    totals = jnp.sum(swapped, axis=0)
    cells = extent // 2
    solution_rows, coarse = call(
        functools.partial(final_kernel, YLOC, rhs),
        [field_shape, jax.ShapeDtypeStruct((rhs * cells, width), f32)],
        *fields,
        totals,
        restriction[0],
        scratch=[pltpu.VMEM((total_rows, width), f32), pltpu.VMEM((total_rows, width), f32)],
        name="final",
    )
    slices = lax.all_gather(coarse, "narrow", axis=0, tiled=True)
    coarse_residual = jnp.transpose(slices.reshape(narrow, rhs, cells, width), (0, 2, 1, 3))
    solution_field = jnp.transpose(solution_rows.reshape(rhs, sites, width), (1, 0, 2))
    return solution_field[None], coarse_residual


def solution(mesh):
    placed = (
        P("narrow", "wide", None, None),
        P("narrow", "wide", None, None, None),
        P("narrow", "wide", None, None),
    )
    return jax.shard_map(
        per_device,
        mesh=mesh,
        in_specs=placed,
        out_specs=(P("narrow", "wide", None, None), P(None, "wide", None, None)),
        check_vma=False,
    )
```

```python
import functools

import jax
import jax.numpy as jnp
from jax import lax
from jax.experimental import pallas as pl
from jax.experimental.pallas import tpu as pltpu
from jax.sharding import PartitionSpec as P


ITERS = 4
YLOC = 2
LY = 16
STEP_SCALE = 0.25
LANES_EACH = 8
SLOT = 32
VMEM_LIMIT = 24 * 1024 * 1024


def tile_starts(rhs):
    starts = list(range(0, rhs - 7, 8))
    if rhs % 8:
        starts.append(rhs - 8)
    return starts


def load_site(ref, site, sites, rhs, by_rhs):
    tiles = []
    for start in tile_starts(rhs):
        if by_rhs:
            tiles.append(ref[pl.ds(start * sites + site, 8, stride=sites), :])
        else:
            tiles.append(ref[site * rhs + start : site * rhs + start + 8, :])
    return jnp.concatenate(tiles, 0)


def store_site(ref, site, sites, rhs, value, by_rhs):
    for at, start in enumerate(tile_starts(rhs)):
        tile = value[8 * at : 8 * at + 8]
        if by_rhs:
            ref[pl.ds(start * sites + site, 8, stride=sites), :] = tile
        else:
            ref[site * rhs + start : site * rhs + start + 8, :] = tile


def operand(block, sign):
    first = block * sign
    second = pltpu.roll(block, block.shape[-1] // 2, 1)
    highs = []
    lows = []
    for part in (first, second):
        high = part.astype(jnp.bfloat16)
        highs.append(high)
        lows.append((part - high.astype(jnp.float32)).astype(jnp.bfloat16))
    return jnp.concatenate(highs + lows, 0)


def lane_sign(width):
    lane = lax.broadcasted_iota(jnp.int32, (1, width), 1)
    return jnp.where(lane < width // 2, 1.0, -1.0).astype(jnp.float32)


def prepare(field_ref, table_ref, first_slot, sites, rhs, by_rhs):
    sign = lane_sign(field_ref.shape[-1])
    for site in range(sites):
        block = load_site(field_ref, site, sites, rhs, by_rhs)
        table_ref[first_slot + site] = operand(block, sign)


def prepare_pair(odd, even_ref, odd_ref, table_ref, first_slot, sites, rhs, by_rhs):
    sign = lane_sign(even_ref.shape[-1])
    for site in range(sites):
        block = jnp.where(
            odd,
            load_site(odd_ref, site, sites, rhs, by_rhs),
            load_site(even_ref, site, sites, rhs, by_rhs),
        )
        table_ref[first_slot + site] = operand(block, sign)


def site_product(slots, blocks):
    rows = slots[0].shape[0] // 4
    left = jnp.concatenate(slots, -1)
    right = jnp.concatenate(blocks, -1)
    total = lax.dot_general(
        left, right, (((1,), (1,)), ((), ())), preferred_element_type=jnp.float32
    )
    real_part = total[0:rows] + total[2 * rows : 3 * rows]
    imag_part = total[rows : 2 * rows] + total[3 * rows : 4 * rows]
    return jnp.concatenate([real_part, imag_part], -1) * STEP_SCALE


def columns_of(total, lanes, slot):
    summed = jnp.sum(total, axis=-1, keepdims=True)
    return jnp.where(lanes == slot, summed, 0.0)


def pair_slots(power):
    slots = []
    at = sum(2 * earlier + 1 for earlier in range(1, power))
    for other in range(power):
        slots.append((other, at, at + 1))
        at += 2
    slots.append((power, at, None))
    return slots


def gram_columns(power, refs, period):
    width = refs[0].shape[-1]
    rows = refs[0].shape[0]
    lanes = lax.broadcasted_iota(jnp.int32, (period, width), 1)
    sign = lane_sign(width)
    out = jnp.zeros((period, width), jnp.float32)
    for other, real_lane, imag_lane in pair_slots(power):
        real_sum = None
        imag_sum = None
        for base in range(0, rows, period):
            mine = refs[power][base : base + period, :]
            theirs = refs[other][base : base + period, :]
            real_term = mine * theirs
            real_sum = real_term if real_sum is None else real_sum + real_term
            if imag_lane is not None:
                turned = pltpu.roll(theirs, width // 2, 1)
                imag_term = mine * turned
                imag_sum = imag_term if imag_sum is None else imag_sum + imag_term
        out = out + columns_of(real_sum, lanes, real_lane)
        if imag_lane is not None:
            out = out + columns_of(imag_sum * sign, lanes, imag_lane)
    return out


def near_sites(hops_ref, table, near_ref, depth, rhs, wrap_z, ready):
    sites = hops_ref.shape[1]
    extent = sites // depth
    for site in range(sites):
        ready(site)
        y, x = divmod(site, extent)
        chosen = [(0, site), (1, y * extent + (x + 1) % extent), (2, y * extent + (x - 1) % extent)]
        if y + 1 < depth:
            chosen.append((3, site + extent))
        if y > 0:
            chosen.append((4, site - extent))
        if wrap_z:
            chosen += [(5, site), (6, site)]
        value = site_product(
            [table[at] for _, at in chosen], [hops_ref[0, site, d] for d, _ in chosen]
        )
        store_site(near_ref, site, sites, rhs, value, False)


def first_near_kernel(depth, rhs, wrap_z, field_hbm, hops_hbm, near_ref, start_ref, hops_ref, table, field_ref, field_sem, hops_sem):
    sites = hops_hbm.shape[1]
    field_copy = pltpu.make_async_copy(field_hbm, field_ref, field_sem)
    field_copy.start()
    copies = [
        pltpu.make_async_copy(hops_hbm.at[0, site], hops_ref.at[0, site], hops_sem.at[site])
        for site in range(sites)
    ]
    for copy in copies:
        copy.start()
    field_copy.wait()
    prepare(field_ref, table, 0, sites, rhs, True)
    for site in range(sites):
        store_site(start_ref, site, sites, rhs, load_site(field_ref, site, sites, rhs, True), False)
    near_sites(hops_ref, table, near_ref, depth, rhs, wrap_z, lambda site: copies[site].wait())


def near_kernel(power, depth, rhs, wrap_z, *refs):
    fields = refs[: power + 1]
    hops_ref, near_ref, gram_ref, table = refs[power + 1 :]
    prepare(fields[power], table, 0, hops_ref.shape[1], rhs, False)
    near_sites(hops_ref, table, near_ref, depth, rhs, wrap_z, lambda site: None)
    gram_ref[...] = gram_columns(power, fields, gram_ref.shape[0])


def far_kernel(depth, rhs, wrap_z, by_rhs, last, *refs):
    near_ref, hops, side_a, side_b, time_a, time_b = refs[:6]
    table = refs[-1]
    extra = refs[6:-1]
    sites = hops.shape[1]
    extent = sites // depth
    ahead = 2 * sites
    behind = ahead + extent
    above = behind + extent
    below = above + sites
    odd_row = lax.rem(lax.axis_index("wide"), 2) == 1
    odd_time = lax.rem(lax.axis_index("narrow"), 2)
    prepare_pair(odd_row, side_a, side_b, table, ahead, extent, rhs, by_rhs)
    prepare_pair(odd_row, side_b, side_a, table, behind, extent, rhs, by_rhs)
    prepare(time_a, table, 0, sites, rhs, by_rhs)
    prepare(time_b, table, sites, sites, rhs, by_rhs)
    if not wrap_z:
        prepare(extra[0], table, above, sites, rhs, by_rhs)
        prepare(extra[1], table, below, sites, rhs, by_rhs)
        extra = extra[2:]
    out_ref = extra[ITERS * 2 - 1] if last else extra[0]
    for site in range(sites):
        y, x = divmod(site, extent)
        chosen = [(7 + odd_time, site), (8 - odd_time, sites + site)]
        if y + 1 == depth:
            chosen.append((3, ahead + x))
        if y == 0:
            chosen.append((4, behind + x))
        if not wrap_z:
            chosen += [(5, above + site), (6, below + site)]
        value = site_product([table[at] for _, at in chosen], [hops[0, site, d] for d, _ in chosen])
        value = value + load_site(near_ref, site, sites, rhs, False)
        store_site(out_ref, site, sites, rhs, value, False)
    if last:
        fields = list(extra[:ITERS]) + [out_ref]
        pack(rhs, fields, extra[ITERS : 2 * ITERS - 1], extra[2 * ITERS])


def pack(rhs, fields, grams, out_ref):
    period, width = grams[0].shape
    total = gram_columns(ITERS, fields, period)
    for gram in grams:
        total = total + gram[...]
    folded = total
    for turn in range(1, period // rhs):
        folded = folded + pltpu.roll(total, turn * rhs, 0)
    per_row = width // SLOT
    row = lax.broadcasted_iota(jnp.int32, (period, width), 0)
    spread = jnp.zeros((period, width), jnp.float32)
    for m in range(per_row):
        part = jnp.where(row % per_row == m, folded, 0.0)
        spread = spread + (pltpu.roll(part, SLOT * m, 1) if m else part)
    for q in range(-(-rhs // per_row)):
        summed = spread[q * per_row : q * per_row + 1]
        for m in range(1, min(per_row, rhs - q * per_row)):
            summed = summed + spread[q * per_row + m : q * per_row + m + 1]
        out_ref[q : q + 1, :] = summed


def cmulc(a, b):
    return (a[0] * b[0] + a[1] * b[1], a[0] * b[1] - a[1] * b[0])


def cmul(a, b):
    return (a[0] * b[0] - a[1] * b[1], a[0] * b[1] + a[1] * b[0])


def cadd(a, b):
    return (a[0] + b[0], a[1] + b[1])


def csub(a, b):
    return (a[0] - b[0], a[1] - b[1])


def step_coefficients(products):
    one = jnp.ones_like(products[1][0][0])

    def times(entry, value):
        if entry[1] is None:
            return (entry[0] * value[0], entry[0] * value[1])
        return cmul(entry, value)

    coeffs = [(one, jnp.zeros_like(one))]
    combined = []
    overlaps = [products[i][0] for i in range(1, ITERS + 1)]
    for step in range(ITERS):
        inner = None
        for i in range(step + 1):
            term = cmulc(coeffs[i], overlaps[i])
            inner = term if inner is None else cadd(inner, term)
        images = []
        for i in range(ITERS):
            value = None
            for j in range(step + 1):
                term = times(products[i + 1][j + 1], coeffs[j])
                value = term if value is None else cadd(value, term)
            images.append(value)
        power = None
        for i in range(step + 1):
            term = coeffs[i][0] * images[i][0] + coeffs[i][1] * images[i][1]
            power = term if power is None else power + term
        alpha = (inner[0] / power, inner[1] / power)
        overlaps = [csub(o, cmul(alpha, im)) for o, im in zip(overlaps, images)]
        scaled = [cmul(alpha, c) for c in coeffs]
        for i, value in enumerate(scaled):
            if i < len(combined):
                combined[i] = cadd(combined[i], value)
            else:
                combined.append(value)
        grown = [coeffs[0]]
        for i in range(1, step + 1):
            grown.append(csub(coeffs[i], scaled[i - 1]))
        grown.append((-scaled[step][0], -scaled[step][1]))
        coeffs = grown
    return coeffs, combined


def final_kernel(depth, rhs, *refs):
    fields = refs[: ITERS + 1]
    packed, restriction = refs[ITERS + 1 : ITERS + 3]
    sol_ref, coarse_ref, res_ref, kept_ref, turn_ref, line_ref, rows_ref = refs[ITERS + 3 :]
    width = fields[0].shape[-1]
    total_rows = fields[0].shape[0]
    period = rhs
    while period % 8:
        period *= 2
    per_row = width // SLOT
    packed_rows = packed.shape[0]
    turn_ref[...] = jnp.zeros_like(turn_ref)
    turn_ref[0:packed_rows, :] = packed[...]
    turned = jnp.transpose(turn_ref[...])
    lane = lax.broadcasted_iota(jnp.int32, (SLOT, width), 1)
    quantities = jnp.zeros((SLOT, width), jnp.float32)
    for m in range(per_row):
        part = turned[SLOT * m : SLOT * m + SLOT]
        moved = pltpu.roll(part, LANES_EACH * m, 1) if m else part
        inside = (lane >= LANES_EACH * m) & (lane < LANES_EACH * m + LANES_EACH)
        quantities = jnp.where(inside, moved, quantities)

    def quantity(at):
        return jnp.broadcast_to(quantities[at : at + 1], (8, width))

    products = [[None] * (ITERS + 1) for _ in range(ITERS + 1)]
    for power in range(1, ITERS + 1):
        for other, real_lane, imag_lane in pair_slots(power):
            re = quantity(real_lane)
            im = quantity(imag_lane) if imag_lane is not None else None
            products[power][other] = (re, im)
            if other and imag_lane is not None:
                products[other][power] = (re, -im)
    coeffs, combined = step_coefficients(products)
    parts = []
    for value in coeffs[1:]:
        parts += [value[0], value[1]]
    for value in combined:
        parts += [value[0] * STEP_SCALE, value[1] * STEP_SCALE]
    line_ref[...] = jnp.zeros_like(line_ref)
    for at, part in enumerate(parts):
        line_ref[at : at + 1, :] = part[0:1]
    turn_ref[...] = jnp.transpose(line_ref[...])
    for r in range(rhs):
        j, m = divmod(r, per_row)
        source = turn_ref[LANES_EACH * m + j : LANES_EACH * m + j + 1, :]
        for at in range(r, period, rhs):
            rows_ref[at : at + 1, :] = source
    columns = rows_ref[...]
    spread = [jnp.broadcast_to(columns[:, at : at + 1], (period, width)) for at in range(len(parts))]
    sign = lane_sign(width)
    for base in range(0, total_rows, period):
        res = fields[0][base : base + period, :]
        res_turn = None
        sol = None
        sol_turn = None
        for i in range(ITERS + 1):
            value = fields[i][base : base + period, :]
            if i:
                at = 2 * (i - 1)
                res = res + spread[at] * value
                term = spread[at + 1] * value
                res_turn = term if res_turn is None else res_turn + term
            if i < ITERS:
                at = 2 * ITERS + 2 * i
                term = spread[at] * value
                sol = term if sol is None else sol + term
                term = spread[at + 1] * value
                sol_turn = term if sol_turn is None else sol_turn + term
        res_ref[base : base + period, :] = res - sign * pltpu.roll(res_turn, width // 2, 1)
        kept_ref[base : base + period, :] = sol - sign * pltpu.roll(sol_turn, width // 2, 1)
    sites = restriction.shape[0]
    extent = sites // depth
    cells = extent // 2
    for cell in range(cells):
        lefts = []
        rights = []
        for y in range(depth):
            for site in (y * extent + 2 * cell, y * extent + 2 * cell + 1):
                block = load_site(res_ref, site, sites, rhs, False)
                turned = pltpu.roll(block, width // 2, 1)
                lefts.append(jnp.concatenate([block * sign, turned], 0))
                rights.append(restriction[site])
        total = lax.dot_general(
            jnp.concatenate(lefts, -1),
            jnp.concatenate(rights, -1),
            (((1,), (1,)), ((), ())),
            precision=lax.Precision.HIGHEST,
            preferred_element_type=jnp.float32,
        )
        half = total.shape[0] // 2
        value = jnp.concatenate([total[:half], total[half:]], -1)
        store_site(coarse_ref, cell, cells, rhs, value, True)
    for site in range(sites):
        store_site(sol_ref, site, sites, rhs, load_site(kept_ref, site, sites, rhs, False), True)


def assemble_kernel(own_ref, *refs):
    out_ref = refs[-1]
    me = lax.axis_index("narrow")
    out_ref[me] = own_ref[...]
    for k, ref in enumerate(refs[:-1]):
        out_ref[jnp.bitwise_xor(me, k + 1)] = ref[...]


def vmem(count):
    return [pl.BlockSpec(memory_space=pltpu.VMEM)] * count


def call(kernel, outs, *args, scratch=(), in_specs=None):
    single = not isinstance(outs, (list, tuple))
    return pl.pallas_call(
        kernel,
        out_shape=outs,
        in_specs=vmem(len(args)) if in_specs is None else in_specs,
        out_specs=pl.BlockSpec(memory_space=pltpu.VMEM) if single else tuple(vmem(len(outs))),
        scratch_shapes=list(scratch),
        compiler_params=pltpu.CompilerParams(vmem_limit_bytes=VMEM_LIMIT),
    )(*args)


def swap_pairs(size, offset, span=None):
    span = size if span is None else span
    pairs = []
    for first in range(0, size, span):
        for i in range(offset, span + offset, 2):
            a, b = first + i % span, first + (i + 1) % span
            pairs += [(a, b), (b, a)]
    return pairs


def per_device(right_side, hop_blocks, restriction):
    sites, rhs, width = right_side.shape[1:]
    extent = sites // YLOC
    rows_y = LY // YLOC
    wide = lax.axis_size("wide")
    narrow = lax.axis_size("narrow")
    wrap_z = wide <= rows_y
    period = rhs
    while period % 8:
        period *= 2
    tile_rows = 8 * len(tile_starts(rhs))
    total_rows = sites * rhs
    half = extent * rhs
    f32 = jnp.float32
    field_shape = jax.ShapeDtypeStruct((total_rows, width), f32)
    gram_shape = jax.ShapeDtypeStruct((period, width), f32)
    hops = hop_blocks

    if rows_y % 2 or narrow % 2 or narrow & (narrow - 1):
        raise ValueError("odd ring")
    up_z = [(i, (i + rows_y) % wide) for i in range(wide)]
    down_z = [(b, a) for a, b in up_z]
    odd_row = lax.axis_index("wide") % 2 == 1

    by_rhs = jnp.transpose(right_side[0], (1, 0, 2))
    field = by_rhs.reshape(total_rows, width)
    first_row = by_rhs[:, :extent].reshape(half, width)
    last_row = by_rhs[:, sites - extent :].reshape(half, width)
    fields = []
    grams = []
    hops = None
    table = pltpu.VMEM((sites, 4 * tile_rows, width), jnp.bfloat16)
    for power in range(ITERS):
        if power:
            field = fields[power]
            first_row = field[:half]
            last_row = field[total_rows - half :]
        up_send = jnp.where(odd_row, first_row, last_row)
        down_send = jnp.where(odd_row, last_row, first_row)
        side_b = lax.ppermute(down_send, "wide", swap_pairs(wide, 1, rows_y))
        side_a = lax.ppermute(up_send, "wide", swap_pairs(wide, 0, rows_y))
        time_b = lax.ppermute(field, "narrow", swap_pairs(narrow, 1))
        time_a = lax.ppermute(field, "narrow", swap_pairs(narrow, 0))
        received = [side_a, side_b, time_a, time_b]
        if not wrap_z:
            received += [lax.ppermute(field, "wide", down_z), lax.ppermute(field, "wide", up_z)]
        if power == 0:
            near, start, hops = call(
                functools.partial(first_near_kernel, YLOC, rhs, wrap_z),
                [field_shape, field_shape, jax.ShapeDtypeStruct(hop_blocks.shape, hop_blocks.dtype)],
                field,
                hop_blocks,
                in_specs=[pl.BlockSpec(memory_space=pl.ANY)] * 2,
                scratch=[
                    table,
                    pltpu.VMEM((total_rows, width), f32),
                    pltpu.SemaphoreType.DMA(()),
                    pltpu.SemaphoreType.DMA((sites,)),
                ],
            )
            fields.append(start)
        else:
            near, gram = call(
                functools.partial(near_kernel, power, YLOC, rhs, wrap_z),
                [field_shape, gram_shape],
                *fields,
                hops,
                scratch=[table],
            )
            grams.append(gram)
        last = power + 1 == ITERS
        slots = 2 * sites + 2 * extent + (0 if wrap_z else 2 * sites)
        per_row = width // SLOT
        packed_rows = -(-rhs // per_row)
        outs = call(
            functools.partial(far_kernel, YLOC, rhs, wrap_z, power == 0, last),
            [field_shape] + ([jax.ShapeDtypeStruct((packed_rows, width), f32)] if last else []),
            near,
            hops,
            *received,
            *(fields + grams if last else []),
            scratch=[pltpu.VMEM((slots, 4 * tile_rows, width), jnp.bfloat16)],
        )
        fields.append(outs[0])
    packed = outs[1]
    copies = jnp.broadcast_to(packed[None], (wide * narrow, packed_rows, width))
    swapped = lax.all_to_all(copies, ("wide", "narrow"), 0, 0)
    totals = jnp.sum(swapped, axis=0)
    cells = extent // 2
    square = pltpu.VMEM((width, width), f32)
    solution_rows, coarse = call(
        functools.partial(final_kernel, YLOC, rhs),
        [field_shape, jax.ShapeDtypeStruct((rhs * cells, width), f32)],
        *fields,
        totals,
        restriction[0],
        scratch=[
            pltpu.VMEM((total_rows, width), f32),
            pltpu.VMEM((total_rows, width), f32),
            square,
            square,
            pltpu.VMEM((period, width), f32),
        ],
    )
    others = []
    for k in range(1, narrow):
        others.append(lax.ppermute(coarse, "narrow", [(i, i ^ k) for i in range(narrow)]))
    slices = call(
        assemble_kernel, jax.ShapeDtypeStruct((narrow,) + coarse.shape, f32), coarse, *others
    )
    coarse_residual = jnp.transpose(slices.reshape(narrow, rhs, cells, width), (0, 2, 1, 3))
    solution_field = jnp.transpose(solution_rows.reshape(rhs, sites, width), (1, 0, 2))
    return solution_field[None], coarse_residual


def solution(mesh):
    placed = (
        P("narrow", "wide", None, None),
        P("narrow", "wide", None, None, None),
        P("narrow", "wide", None, None),
    )
    return jax.shard_map(
        per_device,
        mesh=mesh,
        in_specs=placed,
        out_specs=(P("narrow", "wide", None, None), P(None, "wide", None, None)),
        check_vma=False,
    )
```

```python
import functools

import jax
import jax.numpy as jnp
from jax import lax
from jax.experimental import pallas as pl
from jax.experimental.pallas import tpu as pltpu
from jax.sharding import PartitionSpec as P


ITERS = 4
YLOC = 2
LY = 16
STEP_SCALE = 0.25
LANES_EACH = 8
SLOT = 32
VMEM_LIMIT = 24 * 1024 * 1024


def tile_starts(rhs):
    starts = list(range(0, rhs - 7, 8))
    if rhs % 8:
        starts.append(rhs - 8)
    return starts


def load_site(ref, site, sites, rhs, by_rhs):
    tiles = []
    for start in tile_starts(rhs):
        if by_rhs:
            tiles.append(ref[pl.ds(start * sites + site, 8, stride=sites), :])
        else:
            tiles.append(ref[site * rhs + start : site * rhs + start + 8, :])
    return jnp.concatenate(tiles, 0)


def store_site(ref, site, sites, rhs, value, by_rhs):
    for at, start in enumerate(tile_starts(rhs)):
        tile = value[8 * at : 8 * at + 8]
        if by_rhs:
            ref[pl.ds(start * sites + site, 8, stride=sites), :] = tile
        else:
            ref[site * rhs + start : site * rhs + start + 8, :] = tile


def operand(block, sign):
    first = block * sign
    second = pltpu.roll(block, block.shape[-1] // 2, 1)
    highs = []
    lows = []
    for part in (first, second):
        high = part.astype(jnp.bfloat16)
        highs.append(high)
        lows.append((part - high.astype(jnp.float32)).astype(jnp.bfloat16))
    return jnp.concatenate(highs + lows, 0)


def lane_sign(width):
    lane = lax.broadcasted_iota(jnp.int32, (1, width), 1)
    return jnp.where(lane < width // 2, 1.0, -1.0).astype(jnp.float32)


def prepare(field_ref, table_ref, first_slot, sites, rhs, by_rhs):
    sign = lane_sign(field_ref.shape[-1])
    for site in range(sites):
        block = load_site(field_ref, site, sites, rhs, by_rhs)
        table_ref[first_slot + site] = operand(block, sign)


def prepare_pair(odd, even_ref, odd_ref, table_ref, first_slot, sites, rhs, by_rhs):
    sign = lane_sign(even_ref.shape[-1])
    for site in range(sites):
        block = jnp.where(
            odd,
            load_site(odd_ref, site, sites, rhs, by_rhs),
            load_site(even_ref, site, sites, rhs, by_rhs),
        )
        table_ref[first_slot + site] = operand(block, sign)


def site_product(slots, blocks):
    rows = slots[0].shape[0] // 4
    left = jnp.concatenate(slots, -1)
    right = jnp.concatenate(blocks, -1)
    total = lax.dot_general(
        left, right, (((1,), (1,)), ((), ())), preferred_element_type=jnp.float32
    )
    real_part = total[0:rows] + total[2 * rows : 3 * rows]
    imag_part = total[rows : 2 * rows] + total[3 * rows : 4 * rows]
    return jnp.concatenate([real_part, imag_part], -1) * STEP_SCALE


def columns_of(total, lanes, slot):
    summed = jnp.sum(total, axis=-1, keepdims=True)
    return jnp.where(lanes == slot, summed, 0.0)


def pair_slots(power):
    slots = []
    at = sum(2 * earlier + 1 for earlier in range(1, power))
    for other in range(power):
        slots.append((other, at, at + 1))
        at += 2
    slots.append((power, at, None))
    return slots


def gram_columns(power, refs, period):
    width = refs[0].shape[-1]
    rows = refs[0].shape[0]
    lanes = lax.broadcasted_iota(jnp.int32, (period, width), 1)
    sign = lane_sign(width)
    out = jnp.zeros((period, width), jnp.float32)
    for other, real_lane, imag_lane in pair_slots(power):
        real_sum = None
        imag_sum = None
        for base in range(0, rows, period):
            mine = refs[power][base : base + period, :]
            theirs = refs[other][base : base + period, :]
            real_term = mine * theirs
            real_sum = real_term if real_sum is None else real_sum + real_term
            if imag_lane is not None:
                turned = pltpu.roll(theirs, width // 2, 1)
                imag_term = mine * turned
                imag_sum = imag_term if imag_sum is None else imag_sum + imag_term
        out = out + columns_of(real_sum, lanes, real_lane)
        if imag_lane is not None:
            out = out + columns_of(imag_sum * sign, lanes, imag_lane)
    return out


def near_sites(hops_ref, table, near_ref, depth, rhs, wrap_z, ready):
    sites = hops_ref.shape[1]
    extent = sites // depth
    for site in range(sites):
        ready(site)
        y, x = divmod(site, extent)
        chosen = [(0, site), (1, y * extent + (x + 1) % extent), (2, y * extent + (x - 1) % extent)]
        if y + 1 < depth:
            chosen.append((3, site + extent))
        if y > 0:
            chosen.append((4, site - extent))
        if wrap_z:
            chosen += [(5, site), (6, site)]
        value = site_product(
            [table[at] for _, at in chosen], [hops_ref[0, site, d] for d, _ in chosen]
        )
        store_site(near_ref, site, sites, rhs, value, False)


def open_kernel(extent, right_ref, field_ref, up_ref, down_ref):
    rhs, sites, width = right_ref.shape
    flat = right_ref.reshape(rhs * sites, width)
    for site in range(sites):
        store_site(field_ref, site, sites, rhs, load_site(flat, site, sites, rhs, True), False)
    half = extent * rhs
    choose_sends(field_ref, up_ref, down_ref, half)


def choose_sends(field_ref, up_ref, down_ref, half):
    odd = lax.rem(lax.axis_index("wide"), 2) == 1
    rows = field_ref.shape[0]
    first = field_ref[0:half, :]
    last = field_ref[rows - half : rows, :]
    up_ref[...] = jnp.where(odd, first, last)
    down_ref[...] = jnp.where(odd, last, first)


def first_near_kernel(depth, rhs, wrap_z, field_ref, hops_ref, near_ref, kept_ref, table):
    sites = hops_ref.shape[1]
    prepare(field_ref, table, 0, sites, rhs, False)

    def keep(site):
        kept_ref[0, site] = hops_ref[0, site]

    near_sites(hops_ref, table, near_ref, depth, rhs, wrap_z, keep)


def near_kernel(power, depth, rhs, wrap_z, *refs):
    fields = refs[: power + 1]
    hops_ref, near_ref, gram_ref, table = refs[power + 1 :]
    prepare(fields[power], table, 0, hops_ref.shape[1], rhs, False)
    near_sites(hops_ref, table, near_ref, depth, rhs, wrap_z, lambda site: None)
    gram_ref[...] = gram_columns(power, fields, gram_ref.shape[0])


def far_kernel(depth, rhs, wrap_z, last, *refs):
    near_ref, hops, side_a, side_b, time_a, time_b = refs[:6]
    table = refs[-1]
    extra = refs[6:-1]
    sites = hops.shape[1]
    extent = sites // depth
    ahead = 2 * sites
    behind = ahead + extent
    above = behind + extent
    below = above + sites
    odd_row = lax.rem(lax.axis_index("wide"), 2) == 1
    odd_time = lax.rem(lax.axis_index("narrow"), 2)
    prepare_pair(odd_row, side_a, side_b, table, ahead, extent, rhs, False)
    prepare_pair(odd_row, side_b, side_a, table, behind, extent, rhs, False)
    prepare(time_a, table, 0, sites, rhs, False)
    prepare(time_b, table, sites, sites, rhs, False)
    if not wrap_z:
        prepare(extra[0], table, above, sites, rhs, False)
        prepare(extra[1], table, below, sites, rhs, False)
        extra = extra[2:]
    out_ref = extra[ITERS * 2 - 1] if last else extra[0]
    for site in range(sites):
        y, x = divmod(site, extent)
        chosen = [(7 + odd_time, site), (8 - odd_time, sites + site)]
        if y + 1 == depth:
            chosen.append((3, ahead + x))
        if y == 0:
            chosen.append((4, behind + x))
        if not wrap_z:
            chosen += [(5, above + site), (6, below + site)]
        value = site_product([table[at] for _, at in chosen], [hops[0, site, d] for d, _ in chosen])
        value = value + load_site(near_ref, site, sites, rhs, False)
        store_site(out_ref, site, sites, rhs, value, False)
    if not last:
        choose_sends(out_ref, extra[1], extra[2], extent * rhs)
    else:
        fields = list(extra[:ITERS]) + [out_ref]
        pack(rhs, fields, extra[ITERS : 2 * ITERS - 1], extra[2 * ITERS])


def pack(rhs, fields, grams, out_ref):
    period, width = grams[0].shape
    total = gram_columns(ITERS, fields, period)
    for gram in grams:
        total = total + gram[...]
    folded = total
    for turn in range(1, period // rhs):
        folded = folded + pltpu.roll(total, turn * rhs, 0)
    per_row = width // SLOT
    row = lax.broadcasted_iota(jnp.int32, (period, width), 0)
    spread = jnp.zeros((period, width), jnp.float32)
    for m in range(per_row):
        part = jnp.where(row % per_row == m, folded, 0.0)
        spread = spread + (pltpu.roll(part, SLOT * m, 1) if m else part)
    for q in range(-(-rhs // per_row)):
        summed = spread[q * per_row : q * per_row + 1]
        for m in range(1, min(per_row, rhs - q * per_row)):
            summed = summed + spread[q * per_row + m : q * per_row + m + 1]
        out_ref[q : q + 1, :] = summed


def cmulc(a, b):
    return (a[0] * b[0] + a[1] * b[1], a[0] * b[1] - a[1] * b[0])


def cmul(a, b):
    return (a[0] * b[0] - a[1] * b[1], a[0] * b[1] + a[1] * b[0])


def cadd(a, b):
    return (a[0] + b[0], a[1] + b[1])


def csub(a, b):
    return (a[0] - b[0], a[1] - b[1])


def step_coefficients(products):
    one = jnp.ones_like(products[1][0][0])

    def times(entry, value):
        if entry[1] is None:
            return (entry[0] * value[0], entry[0] * value[1])
        return cmul(entry, value)

    coeffs = [(one, jnp.zeros_like(one))]
    combined = []
    overlaps = [products[i][0] for i in range(1, ITERS + 1)]
    for step in range(ITERS):
        inner = None
        for i in range(step + 1):
            term = cmulc(coeffs[i], overlaps[i])
            inner = term if inner is None else cadd(inner, term)
        images = []
        for i in range(ITERS):
            value = None
            for j in range(step + 1):
                term = times(products[i + 1][j + 1], coeffs[j])
                value = term if value is None else cadd(value, term)
            images.append(value)
        power = None
        for i in range(step + 1):
            term = coeffs[i][0] * images[i][0] + coeffs[i][1] * images[i][1]
            power = term if power is None else power + term
        alpha = (inner[0] / power, inner[1] / power)
        overlaps = [csub(o, cmul(alpha, im)) for o, im in zip(overlaps, images)]
        scaled = [cmul(alpha, c) for c in coeffs]
        for i, value in enumerate(scaled):
            if i < len(combined):
                combined[i] = cadd(combined[i], value)
            else:
                combined.append(value)
        grown = [coeffs[0]]
        for i in range(1, step + 1):
            grown.append(csub(coeffs[i], scaled[i - 1]))
        grown.append((-scaled[step][0], -scaled[step][1]))
        coeffs = grown
    return coeffs, combined


def final_kernel(depth, rhs, *refs):
    fields = refs[: ITERS + 1]
    packed, restriction = refs[ITERS + 1 : ITERS + 3]
    sol_ref, coarse_ref, res_ref, kept_ref, turn_ref, line_ref, rows_ref = refs[ITERS + 3 :]
    width = fields[0].shape[-1]
    total_rows = fields[0].shape[0]
    period = rhs
    while period % 8:
        period *= 2
    per_row = width // SLOT
    packed_rows = packed.shape[0]
    turn_ref[...] = jnp.zeros_like(turn_ref)
    turn_ref[0:packed_rows, :] = packed[...]
    turned = jnp.transpose(turn_ref[...])
    lane = lax.broadcasted_iota(jnp.int32, (SLOT, width), 1)
    quantities = jnp.zeros((SLOT, width), jnp.float32)
    for m in range(per_row):
        part = turned[SLOT * m : SLOT * m + SLOT]
        moved = pltpu.roll(part, LANES_EACH * m, 1) if m else part
        inside = (lane >= LANES_EACH * m) & (lane < LANES_EACH * m + LANES_EACH)
        quantities = jnp.where(inside, moved, quantities)

    def quantity(at):
        return jnp.broadcast_to(quantities[at : at + 1], (8, width))

    products = [[None] * (ITERS + 1) for _ in range(ITERS + 1)]
    for power in range(1, ITERS + 1):
        for other, real_lane, imag_lane in pair_slots(power):
            re = quantity(real_lane)
            im = quantity(imag_lane) if imag_lane is not None else None
            products[power][other] = (re, im)
            if other and imag_lane is not None:
                products[other][power] = (re, -im)
    coeffs, combined = step_coefficients(products)
    parts = []
    for value in coeffs[1:]:
        parts += [value[0], value[1]]
    for value in combined:
        parts += [value[0] * STEP_SCALE, value[1] * STEP_SCALE]
    line_ref[...] = jnp.zeros_like(line_ref)
    for at, part in enumerate(parts):
        line_ref[at : at + 1, :] = part[0:1]
    turn_ref[...] = jnp.transpose(line_ref[...])
    for r in range(rhs):
        j, m = divmod(r, per_row)
        source = turn_ref[LANES_EACH * m + j : LANES_EACH * m + j + 1, :]
        for at in range(r, period, rhs):
            rows_ref[at : at + 1, :] = source
    columns = rows_ref[...]
    spread = [jnp.broadcast_to(columns[:, at : at + 1], (period, width)) for at in range(len(parts))]
    sign = lane_sign(width)
    for base in range(0, total_rows, period):
        res = fields[0][base : base + period, :]
        res_turn = None
        sol = None
        sol_turn = None
        for i in range(ITERS + 1):
            value = fields[i][base : base + period, :]
            if i:
                at = 2 * (i - 1)
                res = res + spread[at] * value
                term = spread[at + 1] * value
                res_turn = term if res_turn is None else res_turn + term
            if i < ITERS:
                at = 2 * ITERS + 2 * i
                term = spread[at] * value
                sol = term if sol is None else sol + term
                term = spread[at + 1] * value
                sol_turn = term if sol_turn is None else sol_turn + term
        res_ref[base : base + period, :] = res - sign * pltpu.roll(res_turn, width // 2, 1)
        kept_ref[base : base + period, :] = sol - sign * pltpu.roll(sol_turn, width // 2, 1)
    sites = restriction.shape[0]
    extent = sites // depth
    cells = extent // 2
    for cell in range(cells):
        lefts = []
        rights = []
        for y in range(depth):
            for site in (y * extent + 2 * cell, y * extent + 2 * cell + 1):
                block = load_site(res_ref, site, sites, rhs, False)
                turned = pltpu.roll(block, width // 2, 1)
                lefts.append(jnp.concatenate([block * sign, turned], 0))
                rights.append(restriction[site])
        total = lax.dot_general(
            jnp.concatenate(lefts, -1),
            jnp.concatenate(rights, -1),
            (((1,), (1,)), ((), ())),
            precision=lax.Precision.HIGHEST,
            preferred_element_type=jnp.float32,
        )
        half = total.shape[0] // 2
        value = jnp.concatenate([total[:half], total[half:]], -1)
        store_site(coarse_ref, cell, cells, rhs, value, True)
    for site in range(sites):
        store_site(sol_ref, site, sites, rhs, load_site(kept_ref, site, sites, rhs, False), True)


def assemble_kernel(own_ref, *refs):
    out_ref = refs[-1]
    me = lax.axis_index("narrow")
    out_ref[me] = own_ref[...]
    for k, ref in enumerate(refs[:-1]):
        out_ref[jnp.bitwise_xor(me, k + 1)] = ref[...]


def vmem(count):
    return [pl.BlockSpec(memory_space=pltpu.VMEM)] * count


def call(kernel, outs, *args, scratch=(), cost=None):
    single = not isinstance(outs, (list, tuple))
    return pl.pallas_call(
        kernel,
        out_shape=outs,
        in_specs=vmem(len(args)),
        out_specs=pl.BlockSpec(memory_space=pltpu.VMEM) if single else tuple(vmem(len(outs))),
        scratch_shapes=list(scratch),
        compiler_params=pltpu.CompilerParams(vmem_limit_bytes=VMEM_LIMIT),
        cost_estimate=cost,
    )(*args)


def swap_pairs(size, offset, span=None):
    span = size if span is None else span
    pairs = []
    for first in range(0, size, span):
        for i in range(offset, span + offset, 2):
            a, b = first + i % span, first + (i + 1) % span
            pairs += [(a, b), (b, a)]
    return pairs


def per_device(right_side, hop_blocks, restriction):
    sites, rhs, width = right_side.shape[1:]
    extent = sites // YLOC
    rows_y = LY // YLOC
    wide = lax.axis_size("wide")
    narrow = lax.axis_size("narrow")
    wrap_z = wide <= rows_y
    period = rhs
    while period % 8:
        period *= 2
    tile_rows = 8 * len(tile_starts(rhs))
    total_rows = sites * rhs
    half = extent * rhs
    f32 = jnp.float32
    field_shape = jax.ShapeDtypeStruct((total_rows, width), f32)
    gram_shape = jax.ShapeDtypeStruct((period, width), f32)
    hops = hop_blocks

    if rows_y % 2 or narrow % 2 or narrow & (narrow - 1):
        raise ValueError("odd ring")
    up_z = [(i, (i + rows_y) % wide) for i in range(wide)]
    down_z = [(b, a) for a, b in up_z]
    half_shape = jax.ShapeDtypeStruct((half, width), f32)
    block_bytes = hop_blocks.size * hop_blocks.dtype.itemsize
    field, up_send, down_send = call(
        functools.partial(open_kernel, extent),
        [field_shape, half_shape, half_shape],
        jnp.transpose(right_side[0], (1, 0, 2)),
        cost=pl.CostEstimate(flops=0, transcendentals=0, bytes_accessed=2 * block_bytes),
    )
    fields = [field]
    grams = []
    hops = None
    table = pltpu.VMEM((sites, 4 * tile_rows, width), jnp.bfloat16)
    for power in range(ITERS):
        side_b = lax.ppermute(down_send, "wide", swap_pairs(wide, 1, rows_y))
        side_a = lax.ppermute(up_send, "wide", swap_pairs(wide, 0, rows_y))
        time_b = lax.ppermute(field, "narrow", swap_pairs(narrow, 1))
        time_a = lax.ppermute(field, "narrow", swap_pairs(narrow, 0))
        received = [side_a, side_b, time_a, time_b]
        if not wrap_z:
            received += [lax.ppermute(field, "wide", down_z), lax.ppermute(field, "wide", up_z)]
        if power == 0:
            near, hops = call(
                functools.partial(first_near_kernel, YLOC, rhs, wrap_z),
                [field_shape, jax.ShapeDtypeStruct(hop_blocks.shape, hop_blocks.dtype)],
                field,
                hop_blocks,
                scratch=[table],
            )
        else:
            near, gram = call(
                functools.partial(near_kernel, power, YLOC, rhs, wrap_z),
                [field_shape, gram_shape],
                *fields,
                hops,
                scratch=[table],
            )
            grams.append(gram)
        last = power + 1 == ITERS
        slots = 2 * sites + 2 * extent + (0 if wrap_z else 2 * sites)
        per_row = width // SLOT
        packed_rows = -(-rhs // per_row)
        outs = call(
            functools.partial(far_kernel, YLOC, rhs, wrap_z, last),
            [field_shape]
            + ([jax.ShapeDtypeStruct((packed_rows, width), f32)] if last else [half_shape] * 2),
            near,
            hops,
            *received,
            *(fields + grams if last else []),
            scratch=[pltpu.VMEM((slots, 4 * tile_rows, width), jnp.bfloat16)],
        )
        field = outs[0]
        fields.append(field)
        if not last:
            up_send, down_send = outs[1:]
    packed = outs[1]
    copies = jnp.broadcast_to(packed[None], (wide * narrow, packed_rows, width))
    swapped = lax.all_to_all(copies, ("wide", "narrow"), 0, 0)
    totals = jnp.sum(swapped, axis=0)
    cells = extent // 2
    square = pltpu.VMEM((width, width), f32)
    solution_rows, coarse = call(
        functools.partial(final_kernel, YLOC, rhs),
        [field_shape, jax.ShapeDtypeStruct((rhs * cells, width), f32)],
        *fields,
        totals,
        restriction[0],
        scratch=[
            pltpu.VMEM((total_rows, width), f32),
            pltpu.VMEM((total_rows, width), f32),
            square,
            square,
            pltpu.VMEM((period, width), f32),
        ],
    )
    others = []
    for k in range(1, narrow):
        others.append(lax.ppermute(coarse, "narrow", [(i, i ^ k) for i in range(narrow)]))
    slices = call(
        assemble_kernel, jax.ShapeDtypeStruct((narrow,) + coarse.shape, f32), coarse, *others
    )
    coarse_residual = jnp.transpose(slices.reshape(narrow, rhs, cells, width), (0, 2, 1, 3))
    solution_field = jnp.transpose(solution_rows.reshape(rhs, sites, width), (1, 0, 2))
    return solution_field[None], coarse_residual


def solution(mesh):
    placed = (
        P("narrow", "wide", None, None),
        P("narrow", "wide", None, None, None),
        P("narrow", "wide", None, None),
    )
    return jax.shard_map(
        per_device,
        mesh=mesh,
        in_specs=placed,
        out_specs=(P("narrow", "wide", None, None), P(None, "wide", None, None)),
        check_vma=False,
    )
```

```python
import functools

import jax
import jax.numpy as jnp
from jax import lax
from jax.experimental import pallas as pl
from jax.experimental.pallas import tpu as pltpu
from jax.sharding import PartitionSpec as P


ITERS = 4
YLOC = 2
LY = 16
STEP_SCALE = 0.25
FIRST_SEND = 3
LANES_EACH = 8
SLOT = 32
VMEM_LIMIT = 24 * 1024 * 1024


def tile_starts(rhs):
    starts = list(range(0, rhs - 7, 8))
    if rhs % 8:
        starts.append(rhs - 8)
    return starts


def load_site(ref, site, sites, rhs, by_rhs):
    tiles = []
    for start in tile_starts(rhs):
        if by_rhs:
            tiles.append(ref[pl.ds(start * sites + site, 8, stride=sites), :])
        else:
            tiles.append(ref[site * rhs + start : site * rhs + start + 8, :])
    return jnp.concatenate(tiles, 0)


def store_site(ref, site, sites, rhs, value, by_rhs):
    for at, start in enumerate(tile_starts(rhs)):
        tile = value[8 * at : 8 * at + 8]
        if by_rhs:
            ref[pl.ds(start * sites + site, 8, stride=sites), :] = tile
        else:
            ref[site * rhs + start : site * rhs + start + 8, :] = tile


def operand(block, sign):
    first = block * sign
    second = pltpu.roll(block, block.shape[-1] // 2, 1)
    highs = []
    lows = []
    for part in (first, second):
        high = part.astype(jnp.bfloat16)
        highs.append(high)
        lows.append((part - high.astype(jnp.float32)).astype(jnp.bfloat16))
    return jnp.concatenate(highs + lows, 0)


def lane_sign(width):
    lane = lax.broadcasted_iota(jnp.int32, (1, width), 1)
    return jnp.where(lane < width // 2, 1.0, -1.0).astype(jnp.float32)


def prepare(field_ref, table_ref, first_slot, sites, rhs, by_rhs):
    sign = lane_sign(field_ref.shape[-1])
    for site in range(sites):
        block = load_site(field_ref, site, sites, rhs, by_rhs)
        table_ref[first_slot + site] = operand(block, sign)


def prepare_pair(odd, even_ref, odd_ref, table_ref, first_slot, sites, rhs, by_rhs):
    sign = lane_sign(even_ref.shape[-1])
    for site in range(sites):
        block = jnp.where(
            odd,
            load_site(odd_ref, site, sites, rhs, by_rhs),
            load_site(even_ref, site, sites, rhs, by_rhs),
        )
        table_ref[first_slot + site] = operand(block, sign)


def site_product(slots, blocks):
    rows = slots[0].shape[0] // 4
    left = jnp.concatenate(slots, -1)
    right = jnp.concatenate(blocks, -1)
    total = lax.dot_general(
        left, right, (((1,), (1,)), ((), ())), preferred_element_type=jnp.float32
    )
    real_part = total[0:rows] + total[2 * rows : 3 * rows]
    imag_part = total[rows : 2 * rows] + total[3 * rows : 4 * rows]
    return jnp.concatenate([real_part, imag_part], -1) * STEP_SCALE


def columns_of(total, lanes, slot):
    summed = jnp.sum(total, axis=-1, keepdims=True)
    return jnp.where(lanes == slot, summed, 0.0)


def pair_slots(power):
    slots = []
    at = sum(2 * earlier + 1 for earlier in range(1, power))
    for other in range(power):
        slots.append((other, at, at + 1))
        at += 2
    slots.append((power, at, None))
    return slots


def gram_columns(power, refs, period):
    width = refs[0].shape[-1]
    rows = refs[0].shape[0]
    lanes = lax.broadcasted_iota(jnp.int32, (period, width), 1)
    sign = lane_sign(width)
    out = jnp.zeros((period, width), jnp.float32)
    for other, real_lane, imag_lane in pair_slots(power):
        real_sum = None
        imag_sum = None
        for base in range(0, rows, period):
            mine = refs[power][base : base + period, :]
            theirs = refs[other][base : base + period, :]
            real_term = mine * theirs
            real_sum = real_term if real_sum is None else real_sum + real_term
            if imag_lane is not None:
                turned = pltpu.roll(theirs, width // 2, 1)
                imag_term = mine * turned
                imag_sum = imag_term if imag_sum is None else imag_sum + imag_term
        out = out + columns_of(real_sum, lanes, real_lane)
        if imag_lane is not None:
            out = out + columns_of(imag_sum * sign, lanes, imag_lane)
    return out


def restrict_field(field_ref, restriction, depth, rhs, out_ref, base):
    width = field_ref.shape[-1]
    sign = lane_sign(width)
    extent = restriction.shape[0] // depth
    for cell in range(extent // 2):
        lefts = []
        rights = []
        for y in range(depth):
            for site in (y * extent + 2 * cell, y * extent + 2 * cell + 1):
                block = load_site(field_ref, site, 0, rhs, False)
                turned = pltpu.roll(block, width // 2, 1)
                lefts.append(jnp.concatenate([block * sign, turned], 0))
                rights.append(restriction[site])
        total = lax.dot_general(
            jnp.concatenate(lefts, -1),
            jnp.concatenate(rights, -1),
            (((1,), (1,)), ((), ())),
            precision=lax.Precision.HIGHEST,
            preferred_element_type=jnp.float32,
        )
        half = total.shape[0] // 2
        value = jnp.concatenate([total[:half], total[half:]], -1)
        for at, start in enumerate(tile_starts(rhs)):
            row = base + cell * rhs + start
            out_ref[row : row + 8, :] = value[8 * at : 8 * at + 8]


def near_sites(hops_ref, table, near_ref, depth, rhs, wrap_z, ready):
    sites = hops_ref.shape[1]
    extent = sites // depth
    for site in range(sites):
        ready(site)
        y, x = divmod(site, extent)
        chosen = [(0, site), (1, y * extent + (x + 1) % extent), (2, y * extent + (x - 1) % extent)]
        if y + 1 < depth:
            chosen.append((3, site + extent))
        if y > 0:
            chosen.append((4, site - extent))
        if wrap_z:
            chosen += [(5, site), (6, site)]
        value = site_product(
            [table[at] for _, at in chosen], [hops_ref[0, site, d] for d, _ in chosen]
        )
        store_site(near_ref, site, sites, rhs, value, False)


def open_kernel(extent, right_ref, field_ref, up_ref, down_ref):
    rhs, sites, width = right_ref.shape
    flat = right_ref.reshape(rhs * sites, width)
    for site in range(sites):
        store_site(field_ref, site, sites, rhs, load_site(flat, site, sites, rhs, True), False)
    half = extent * rhs
    choose_sends(field_ref, up_ref, down_ref, half)


def choose_sends(field_ref, up_ref, down_ref, half):
    odd = lax.rem(lax.axis_index("wide"), 2) == 1
    rows = field_ref.shape[0]
    first = field_ref[0:half, :]
    last = field_ref[rows - half : rows, :]
    up_ref[...] = jnp.where(odd, first, last)
    down_ref[...] = jnp.where(odd, last, first)


def near_kernel(power, depth, rhs, wrap_z, *refs):
    fields = refs[: power + 1]
    hops_ref = refs[power + 1]
    if power:
        near_ref, coarse_ref, other_ref, table = refs[-4:]
    else:
        near_ref, other_ref, table = refs[-3:]
    prepare(fields[power], table, 0, hops_ref.shape[1], rhs, False)

    def keep(site):
        if power == 0:
            other_ref[0, site] = hops_ref[0, site]

    near_sites(hops_ref, table, near_ref, depth, rhs, wrap_z, keep)
    if power:
        restriction = refs[power + 2]
        earlier = refs[power + 3 : -4]
        base = 0
        for ref in earlier:
            coarse_ref[base : base + ref.shape[0], :] = ref[...]
            base += ref.shape[0]
        for field_ref in fields if power == 1 else fields[power:]:
            restrict_field(field_ref, restriction, depth, rhs, coarse_ref, base)
            base += restriction.shape[0] // depth // 2 * rhs
        other_ref[...] = gram_columns(power, fields, other_ref.shape[0])


def far_kernel(depth, rhs, wrap_z, last, *refs):
    near_ref, hops, side_a, side_b, time_a, time_b = refs[:6]
    table = refs[-1]
    extra = refs[6:-1]
    sites = hops.shape[1]
    extent = sites // depth
    ahead = 2 * sites
    behind = ahead + extent
    above = behind + extent
    below = above + sites
    odd_row = lax.rem(lax.axis_index("wide"), 2) == 1
    odd_time = lax.rem(lax.axis_index("narrow"), 2)
    prepare_pair(odd_row, side_a, side_b, table, ahead, extent, rhs, False)
    prepare_pair(odd_row, side_b, side_a, table, behind, extent, rhs, False)
    prepare(time_a, table, 0, sites, rhs, False)
    prepare(time_b, table, sites, sites, rhs, False)
    if not wrap_z:
        prepare(extra[0], table, above, sites, rhs, False)
        prepare(extra[1], table, below, sites, rhs, False)
        extra = extra[2:]
    out_ref = extra[ITERS * 2 - 1] if last else extra[0]
    for site in range(sites):
        y, x = divmod(site, extent)
        chosen = [(7 + odd_time, site), (8 - odd_time, sites + site)]
        if y + 1 == depth:
            chosen.append((3, ahead + x))
        if y == 0:
            chosen.append((4, behind + x))
        if not wrap_z:
            chosen += [(5, above + site), (6, below + site)]
        value = site_product([table[at] for _, at in chosen], [hops[0, site, d] for d, _ in chosen])
        value = value + load_site(near_ref, site, sites, rhs, False)
        store_site(out_ref, site, sites, rhs, value, False)
    if not last:
        choose_sends(out_ref, extra[1], extra[2], extent * rhs)
    else:
        fields = list(extra[:ITERS]) + [out_ref]
        pack(rhs, fields, extra[ITERS : 2 * ITERS - 1], extra[2 * ITERS])


def pack(rhs, fields, grams, out_ref):
    period, width = grams[0].shape
    total = gram_columns(ITERS, fields, period)
    for gram in grams:
        total = total + gram[...]
    folded = total
    for turn in range(1, period // rhs):
        folded = folded + pltpu.roll(total, turn * rhs, 0)
    per_row = width // SLOT
    row = lax.broadcasted_iota(jnp.int32, (period, width), 0)
    spread = jnp.zeros((period, width), jnp.float32)
    for m in range(per_row):
        part = jnp.where(row % per_row == m, folded, 0.0)
        spread = spread + (pltpu.roll(part, SLOT * m, 1) if m else part)
    for q in range(-(-rhs // per_row)):
        summed = spread[q * per_row : q * per_row + 1]
        for m in range(1, min(per_row, rhs - q * per_row)):
            summed = summed + spread[q * per_row + m : q * per_row + m + 1]
        for copy in range(out_ref.shape[0]):
            out_ref[copy, q : q + 1, :] = summed


def tail_kernel(depth, rhs, field_ref, restriction, coarse_ref):
    restrict_field(field_ref, restriction, depth, rhs, coarse_ref, 0)


def cmulc(a, b):
    return (a[0] * b[0] + a[1] * b[1], a[0] * b[1] - a[1] * b[0])


def cmul(a, b):
    return (a[0] * b[0] - a[1] * b[1], a[0] * b[1] + a[1] * b[0])


def cadd(a, b):
    return (a[0] + b[0], a[1] + b[1])


def csub(a, b):
    return (a[0] - b[0], a[1] - b[1])


def step_coefficients(products):
    one = jnp.ones_like(products[1][0][0])

    def times(entry, value):
        if entry[1] is None:
            return (entry[0] * value[0], entry[0] * value[1])
        return cmul(entry, value)

    coeffs = [(one, jnp.zeros_like(one))]
    combined = []
    overlaps = [products[i][0] for i in range(1, ITERS + 1)]
    for step in range(ITERS):
        inner = None
        for i in range(step + 1):
            term = cmulc(coeffs[i], overlaps[i])
            inner = term if inner is None else cadd(inner, term)
        images = []
        for i in range(ITERS):
            value = None
            for j in range(step + 1):
                term = times(products[i + 1][j + 1], coeffs[j])
                value = term if value is None else cadd(value, term)
            images.append(value)
        power = None
        for i in range(step + 1):
            term = coeffs[i][0] * images[i][0] + coeffs[i][1] * images[i][1]
            power = term if power is None else power + term
        alpha = (inner[0] / power, inner[1] / power)
        overlaps = [csub(o, cmul(alpha, im)) for o, im in zip(overlaps, images)]
        scaled = [cmul(alpha, c) for c in coeffs]
        for i, value in enumerate(scaled):
            if i < len(combined):
                combined[i] = cadd(combined[i], value)
            else:
                combined.append(value)
        grown = [coeffs[0]]
        for i in range(1, step + 1):
            grown.append(csub(coeffs[i], scaled[i - 1]))
        grown.append((-scaled[step][0], -scaled[step][1]))
        coeffs = grown
    return coeffs, combined


def final_kernel(sites, rhs, groups, *refs):
    fields = refs[:ITERS]
    packed = refs[ITERS]
    coarse_refs = refs[ITERS + 1 : -7]
    sol_ref, coarse_ref, kept_ref, slice_ref, turn_ref, line_ref, rows_ref = refs[-7:]
    width = fields[0].shape[-1]
    total_rows = fields[0].shape[0]
    period = rhs
    while period % 8:
        period *= 2
    per_row = width // SLOT
    packed_rows = packed.shape[0]
    turn_ref[...] = jnp.zeros_like(turn_ref)
    turn_ref[0:packed_rows, :] = packed[...]
    turned = jnp.transpose(turn_ref[...])
    lane = lax.broadcasted_iota(jnp.int32, (SLOT, width), 1)
    quantities = jnp.zeros((SLOT, width), jnp.float32)
    for m in range(per_row):
        part = turned[SLOT * m : SLOT * m + SLOT]
        moved = pltpu.roll(part, LANES_EACH * m, 1) if m else part
        inside = (lane >= LANES_EACH * m) & (lane < LANES_EACH * m + LANES_EACH)
        quantities = jnp.where(inside, moved, quantities)

    def quantity(at):
        return jnp.broadcast_to(quantities[at : at + 1], (8, width))

    products = [[None] * (ITERS + 1) for _ in range(ITERS + 1)]
    for power in range(1, ITERS + 1):
        for other, real_lane, imag_lane in pair_slots(power):
            re = quantity(real_lane)
            im = quantity(imag_lane) if imag_lane is not None else None
            products[power][other] = (re, im)
            if other and imag_lane is not None:
                products[other][power] = (re, -im)
    coeffs, combined = step_coefficients(products)
    parts = []
    for value in coeffs[1:]:
        parts += [value[0], value[1]]
    for value in combined:
        parts += [value[0] * STEP_SCALE, value[1] * STEP_SCALE]
    line_ref[...] = jnp.zeros_like(line_ref)
    for at, part in enumerate(parts):
        line_ref[at : at + 1, :] = part[0:1]
    turn_ref[...] = jnp.transpose(line_ref[...])
    for r in range(rhs):
        j, m = divmod(r, per_row)
        source = turn_ref[LANES_EACH * m + j : LANES_EACH * m + j + 1, :]
        for at in range(r, period, rhs):
            rows_ref[at : at + 1, :] = source
    columns = rows_ref[...]
    spread = [jnp.broadcast_to(columns[:, at : at + 1], (period, width)) for at in range(len(parts))]
    sign = lane_sign(width)
    half_width = width // 2
    for base in range(0, total_rows, period):
        straight = None
        across = None
        for i in range(ITERS):
            value = fields[i][base : base + period, :]
            at = 2 * ITERS + 2 * i
            terms = (spread[at] * value, spread[at + 1] * value)
            straight = terms[0] if straight is None else straight + terms[0]
            across = terms[1] if across is None else across + terms[1]
        kept_ref[base : base + period, :] = straight - sign * pltpu.roll(across, half_width, 1)
    for site in range(sites):
        store_site(sol_ref, site, sites, rhs, load_site(kept_ref, site, sites, rhs, False), True)
    me = lax.axis_index("narrow")
    slice_rows = slice_ref.shape[0]
    cells = slice_rows // rhs
    count = len(groups)
    for k in range(len(coarse_refs) // count):
        mine = coarse_refs[k * count : (k + 1) * count]
        placed = [(ref, part) for ref, stack in zip(mine, groups) for part in range(stack)]
        for base in range(0, slice_rows, period):
            straight = None
            across = None
            for i, (ref, part) in enumerate(placed):
                row = part * slice_rows + base
                value = ref[row : row + period, :]
                if i == 0:
                    straight = value
                    continue
                terms = (spread[2 * i - 2] * value, spread[2 * i - 1] * value)
                straight = straight + terms[0]
                across = terms[1] if across is None else across + terms[1]
            slice_ref[base : base + period, :] = straight - sign * pltpu.roll(across, half_width, 1)
        target = coarse_ref.at[jnp.bitwise_xor(me, k)]
        for cell in range(cells):
            store_site(target, cell, cells, rhs, load_site(slice_ref, cell, cells, rhs, False), True)


def vmem(count):
    return [pl.BlockSpec(memory_space=pltpu.VMEM)] * count


def call(kernel, outs, *args, scratch=(), cost=None):
    single = not isinstance(outs, (list, tuple))
    return pl.pallas_call(
        kernel,
        out_shape=outs,
        in_specs=vmem(len(args)),
        out_specs=pl.BlockSpec(memory_space=pltpu.VMEM) if single else tuple(vmem(len(outs))),
        scratch_shapes=list(scratch),
        compiler_params=pltpu.CompilerParams(vmem_limit_bytes=VMEM_LIMIT),
        cost_estimate=cost,
    )(*args)


def swap_pairs(size, offset, span=None):
    span = size if span is None else span
    pairs = []
    for first in range(0, size, span):
        for i in range(offset, span + offset, 2):
            a, b = first + i % span, first + (i + 1) % span
            pairs += [(a, b), (b, a)]
    return pairs


def per_device(right_side, hop_blocks, restriction):
    sites, rhs, width = right_side.shape[1:]
    extent = sites // YLOC
    rows_y = LY // YLOC
    wide = lax.axis_size("wide")
    narrow = lax.axis_size("narrow")
    wrap_z = wide <= rows_y
    period = rhs
    while period % 8:
        period *= 2
    tile_rows = 8 * len(tile_starts(rhs))
    total_rows = sites * rhs
    half = extent * rhs
    f32 = jnp.float32
    field_shape = jax.ShapeDtypeStruct((total_rows, width), f32)
    gram_shape = jax.ShapeDtypeStruct((period, width), f32)
    hops = hop_blocks

    if rows_y % 2 or narrow % 2 or narrow & (narrow - 1):
        raise ValueError("odd ring")
    up_z = [(i, (i + rows_y) % wide) for i in range(wide)]
    down_z = [(b, a) for a, b in up_z]
    half_shape = jax.ShapeDtypeStruct((half, width), f32)
    block_bytes = hop_blocks.size * hop_blocks.dtype.itemsize
    field, up_send, down_send = call(
        functools.partial(open_kernel, extent),
        [field_shape, half_shape, half_shape],
        jnp.transpose(right_side[0], (1, 0, 2)),
        cost=pl.CostEstimate(flops=0, transcendentals=0, bytes_accessed=2 * block_bytes),
    )
    fields = [field]
    grams = []
    waiting = []
    sent = []
    groups = []
    cells = extent // 2
    coarse_rows = cells * rhs

    def to_all_times(value):
        arrived = [value]
        for k in range(narrow - 1, 0, -1):
            arrived.insert(1, lax.ppermute(value, "narrow", [(i, i ^ k) for i in range(narrow)]))
        return arrived

    hops = None
    table = pltpu.VMEM((sites, 4 * tile_rows, width), jnp.bfloat16)
    for power in range(ITERS):
        side_b = lax.ppermute(down_send, "wide", swap_pairs(wide, 1, rows_y))
        side_a = lax.ppermute(up_send, "wide", swap_pairs(wide, 0, rows_y))
        time_b = lax.ppermute(field, "narrow", swap_pairs(narrow, 1))
        time_a = lax.ppermute(field, "narrow", swap_pairs(narrow, 0))
        received = [side_a, side_b, time_a, time_b]
        if not wrap_z:
            received += [lax.ppermute(field, "wide", down_z), lax.ppermute(field, "wide", up_z)]
        if power == 0:
            near, hops = call(
                functools.partial(near_kernel, power, YLOC, rhs, wrap_z),
                [field_shape, jax.ShapeDtypeStruct(hop_blocks.shape, hop_blocks.dtype)],
                field,
                hop_blocks,
                scratch=[table],
            )
        else:
            stacked = sum(ref.shape[0] for ref in waiting) + coarse_rows * (2 if power == 1 else 1)
            near, coarse, gram = call(
                functools.partial(near_kernel, power, YLOC, rhs, wrap_z),
                [field_shape, jax.ShapeDtypeStruct((stacked, width), f32), gram_shape],
                *fields,
                hops,
                restriction[0],
                *waiting,
                scratch=[table],
            )
            grams.append(gram)
            waiting = [coarse]
            if power >= FIRST_SEND:
                groups.append(stacked // coarse_rows)
                sent.append(to_all_times(coarse))
                waiting = []
        last = power + 1 == ITERS
        slots = 2 * sites + 2 * extent + (0 if wrap_z else 2 * sites)
        per_row = width // SLOT
        packed_rows = -(-rhs // per_row)
        outs = call(
            functools.partial(far_kernel, YLOC, rhs, wrap_z, last),
            [field_shape]
            + (
                [jax.ShapeDtypeStruct((wide * narrow, packed_rows, width), f32)]
                if last
                else [half_shape] * 2
            ),
            near,
            hops,
            *received,
            *(fields + grams if last else []),
            scratch=[pltpu.VMEM((slots, 4 * tile_rows, width), jnp.bfloat16)],
        )
        field = outs[0]
        fields.append(field)
        if not last:
            up_send, down_send = outs[1:]
        else:
            swapped = lax.all_to_all(outs[1], ("wide", "narrow"), 0, 0)
            coarse = call(
                functools.partial(tail_kernel, YLOC, rhs),
                jax.ShapeDtypeStruct((coarse_rows, width), f32),
                field,
                restriction[0],
            )
            groups.append(1)
            sent.append(to_all_times(coarse))
    totals = jnp.sum(swapped, axis=0)
    square = pltpu.VMEM((width, width), f32)
    solution_rows, slices = call(
        functools.partial(final_kernel, sites, rhs, tuple(groups)),
        [field_shape, jax.ShapeDtypeStruct((narrow, coarse_rows, width), f32)],
        *fields[:ITERS],
        totals,
        *[arrived[k] for k in range(narrow) for arrived in sent],
        scratch=[
            pltpu.VMEM((total_rows, width), f32),
            pltpu.VMEM((coarse_rows, width), f32),
            square,
            square,
            pltpu.VMEM((period, width), f32),
        ],
    )
    coarse_residual = jnp.transpose(slices.reshape(narrow, rhs, cells, width), (0, 2, 1, 3))
    solution_field = jnp.transpose(solution_rows.reshape(rhs, sites, width), (1, 0, 2))
    return solution_field[None], coarse_residual


def solution(mesh):
    placed = (
        P("narrow", "wide", None, None),
        P("narrow", "wide", None, None, None),
        P("narrow", "wide", None, None),
    )
    return jax.shard_map(
        per_device,
        mesh=mesh,
        in_specs=placed,
        out_specs=(P("narrow", "wide", None, None), P(None, "wide", None, None)),
        check_vma=False,
    )
```

```python
import functools

import jax
import jax.numpy as jnp
from jax import lax
from jax.experimental import pallas as pl
from jax.experimental.pallas import tpu as pltpu
from jax.sharding import PartitionSpec as P


ITERS = 4
YLOC = 2
LY = 16
STEP_SCALE = 0.25
FIRST_SEND = 3
LANES_EACH = 8
SLOT = 32
VMEM_LIMIT = 24 * 1024 * 1024


def tile_starts(rhs):
    starts = list(range(0, rhs - 7, 8))
    if rhs % 8:
        starts.append(rhs - 8)
    return starts


def load_site(ref, site, sites, rhs, by_rhs):
    tiles = []
    for start in tile_starts(rhs):
        if by_rhs:
            tiles.append(ref[pl.ds(start * sites + site, 8, stride=sites), :])
        else:
            tiles.append(ref[site * rhs + start : site * rhs + start + 8, :])
    return jnp.concatenate(tiles, 0)


def store_site(ref, site, sites, rhs, value, by_rhs):
    for at, start in enumerate(tile_starts(rhs)):
        tile = value[8 * at : 8 * at + 8]
        if by_rhs:
            ref[pl.ds(start * sites + site, 8, stride=sites), :] = tile
        else:
            ref[site * rhs + start : site * rhs + start + 8, :] = tile


def operand(block, sign):
    first = block * sign
    second = pltpu.roll(block, block.shape[-1] // 2, 1)
    highs = []
    lows = []
    for part in (first, second):
        high = part.astype(jnp.bfloat16)
        highs.append(high)
        lows.append((part - high.astype(jnp.float32)).astype(jnp.bfloat16))
    return jnp.concatenate(highs + lows, 0)


def split_operand(block):
    high = block.astype(jnp.bfloat16)
    low = (block - high.astype(jnp.float32)).astype(jnp.bfloat16)
    return jnp.concatenate([high, low], 0)


def lane_sign(width):
    lane = lax.broadcasted_iota(jnp.int32, (1, width), 1)
    return jnp.where(lane < width // 2, 1.0, -1.0).astype(jnp.float32)


def prepare(field_ref, table_ref, first_slot, sites, rhs, dense=False):
    sign = lane_sign(field_ref.shape[-1])
    for site in range(sites):
        block = load_site(field_ref, site, sites, rhs, False)
        table_ref[first_slot + site] = split_operand(block) if dense else operand(block, sign)


def prepare_pair(odd, even_ref, odd_ref, table_ref, first_slot, sites, rhs, dense):
    sign = lane_sign(even_ref.shape[-1])
    for site in range(sites):
        block = jnp.where(
            odd,
            load_site(odd_ref, site, sites, rhs, False),
            load_site(even_ref, site, sites, rhs, False),
        )
        table_ref[first_slot + site] = split_operand(block) if dense else operand(block, sign)


def site_product(slots, blocks):
    rows = slots[0].shape[0] // 4
    left = jnp.concatenate(slots, -1)
    right = jnp.concatenate(blocks, -1)
    total = lax.dot_general(
        left, right, (((1,), (1,)), ((), ())), preferred_element_type=jnp.float32
    )
    real_part = total[0:rows] + total[2 * rows : 3 * rows]
    imag_part = total[rows : 2 * rows] + total[3 * rows : 4 * rows]
    return jnp.concatenate([real_part, imag_part], -1) * STEP_SCALE


def columns_of(total, lanes, slot):
    summed = jnp.sum(total, axis=-1, keepdims=True)
    return jnp.where(lanes == slot, summed, 0.0)


def pair_slots(power):
    slots = []
    at = sum(2 * earlier + 1 for earlier in range(1, power))
    for other in range(power):
        slots.append((other, at, at + 1))
        at += 2
    slots.append((power, at, None))
    return slots


def gram_columns(power, refs, period):
    width = refs[0].shape[-1]
    rows = refs[0].shape[0]
    lanes = lax.broadcasted_iota(jnp.int32, (period, width), 1)
    sign = lane_sign(width)
    out = jnp.zeros((period, width), jnp.float32)
    for other, real_lane, imag_lane in pair_slots(power):
        real_sum = None
        imag_sum = None
        for base in range(0, rows, period):
            mine = refs[power][base : base + period, :]
            theirs = refs[other][base : base + period, :]
            real_term = mine * theirs
            real_sum = real_term if real_sum is None else real_sum + real_term
            if imag_lane is not None:
                turned = pltpu.roll(theirs, width // 2, 1)
                imag_term = mine * turned
                imag_sum = imag_term if imag_sum is None else imag_sum + imag_term
        out = out + columns_of(real_sum, lanes, real_lane)
        if imag_lane is not None:
            out = out + columns_of(imag_sum * sign, lanes, imag_lane)
    return out


def restrict_field(field_ref, restriction, depth, rhs, out_ref, base):
    width = field_ref.shape[-1]
    sign = lane_sign(width)
    extent = restriction.shape[0] // depth
    for cell in range(extent // 2):
        lefts = []
        rights = []
        for y in range(depth):
            for site in (y * extent + 2 * cell, y * extent + 2 * cell + 1):
                block = load_site(field_ref, site, 0, rhs, False)
                turned = pltpu.roll(block, width // 2, 1)
                lefts.append(jnp.concatenate([block * sign, turned], 0))
                rights.append(restriction[site])
        total = lax.dot_general(
            jnp.concatenate(lefts, -1),
            jnp.concatenate(rights, -1),
            (((1,), (1,)), ((), ())),
            precision=lax.Precision.HIGHEST,
            preferred_element_type=jnp.float32,
        )
        half = total.shape[0] // 2
        value = jnp.concatenate([total[:half], total[half:]], -1)
        for at, start in enumerate(tile_starts(rhs)):
            row = base + cell * rhs + start
            out_ref[row : row + 8, :] = value[8 * at : 8 * at + 8]


def dense_product(slots, blocks):
    total = lax.dot_general(
        jnp.concatenate(slots, -1), blocks, (((1,), (0,)), ((), ())), preferred_element_type=jnp.float32
    )
    rows = total.shape[0] // 2
    return total[:rows] + total[rows:]


def far_list(site, sites, depth, wrap_z, odd_time):
    extent = sites // depth
    ahead = 2 * sites
    behind = ahead + extent
    above = behind + extent
    below = above + sites
    y, x = divmod(site, extent)
    chosen = [(7 + odd_time, site), (8 - odd_time, sites + site)]
    if y + 1 == depth:
        chosen.append((3, ahead + x))
    if y == 0:
        chosen.append((4, behind + x))
    if not wrap_z:
        chosen += [(5, above + site), (6, below + site)]
    return chosen


def build_dense(hops_ref, dense_ref, depth, wrap_z):
    sites, _, half, width = hops_ref.shape[1:]
    odd_time = lax.rem(lax.axis_index("narrow"), 2)
    row = lax.broadcasted_iota(jnp.int32, (width, 2 * width), 0)
    col = lax.broadcasted_iota(jnp.int32, (width, 2 * width), 1)
    signed = jnp.where(row < half, STEP_SCALE, -STEP_SCALE)
    swapped = jnp.where(row < half, row + half, row - half) + width
    select = jnp.where(col == row, signed, jnp.where(col == swapped, STEP_SCALE, 0.0))
    select = select.astype(jnp.bfloat16)
    empty = jnp.zeros((half, width), jnp.bfloat16)
    for site in range(sites):
        for at, (d, _) in enumerate(far_list(site, sites, depth, wrap_z, odd_time)):
            block = hops_ref[0, site, d]
            pair = jnp.concatenate(
                [jnp.concatenate([block, empty], -1), jnp.concatenate([empty, block], -1)], 0
            )
            dense = lax.dot_general(
                select, pair, (((1,), (1,)), ((), ())), preferred_element_type=jnp.float32
            )
            dense_ref[site, at * width : (at + 1) * width, :] = dense.astype(jnp.bfloat16)


def near_sites(hops_ref, table, near_ref, depth, rhs, wrap_z, ready):
    sites = hops_ref.shape[1]
    extent = sites // depth
    for site in range(sites):
        ready(site)
        y, x = divmod(site, extent)
        chosen = [(0, site), (1, y * extent + (x + 1) % extent), (2, y * extent + (x - 1) % extent)]
        if y + 1 < depth:
            chosen.append((3, site + extent))
        if y > 0:
            chosen.append((4, site - extent))
        if wrap_z:
            chosen += [(5, site), (6, site)]
        value = site_product(
            [table[at] for _, at in chosen], [hops_ref[0, site, d] for d, _ in chosen]
        )
        store_site(near_ref, site, sites, rhs, value, False)


def open_kernel(extent, right_ref, field_ref, up_ref, down_ref):
    rhs, sites, width = right_ref.shape
    flat = right_ref.reshape(rhs * sites, width)
    for site in range(sites):
        store_site(field_ref, site, sites, rhs, load_site(flat, site, sites, rhs, True), False)
    half = extent * rhs
    choose_sends(field_ref, up_ref, down_ref, half)


def choose_sends(field_ref, up_ref, down_ref, half):
    odd = lax.rem(lax.axis_index("wide"), 2) == 1
    rows = field_ref.shape[0]
    first = field_ref[0:half, :]
    last = field_ref[rows - half : rows, :]
    up_ref[...] = jnp.where(odd, first, last)
    down_ref[...] = jnp.where(odd, last, first)


def near_kernel(power, depth, rhs, wrap_z, *refs):
    fields = refs[: power + 1]
    hops_ref = refs[power + 1]
    near_ref, other_ref, table = refs[-3:] if power == 0 else (refs[-4], refs[-2], refs[-1])
    prepare(fields[power], table, 0, hops_ref.shape[1], rhs)

    def keep(site):
        if power == 0:
            other_ref[0, site] = hops_ref[0, site]

    near_sites(hops_ref, table, near_ref, depth, rhs, wrap_z, keep)
    if power == 1:
        build_dense(hops_ref, refs[-3], depth, wrap_z)
    elif power > 1:
        restriction, coarse_ref = refs[power + 2], refs[-3]
        base = 0
        for ref in refs[power + 3 : -4]:
            coarse_ref[base : base + ref.shape[0], :] = ref[...]
            base += ref.shape[0]
        for field_ref in fields if power == 2 else fields[power:]:
            restrict_field(field_ref, restriction, depth, rhs, coarse_ref, base)
            base += restriction.shape[0] // depth // 2 * rhs
    if power:
        other_ref[...] = gram_columns(power, fields, other_ref.shape[0])


def far_kernel(depth, rhs, wrap_z, dense, last, *refs):
    near_ref, blocks, side_a, side_b, time_a, time_b = refs[:6]
    table = refs[-1]
    extra = refs[6:-1]
    extent = side_a.shape[0] // rhs
    sites = extent * depth
    ahead = 2 * sites
    odd_row = lax.rem(lax.axis_index("wide"), 2) == 1
    odd_time = lax.rem(lax.axis_index("narrow"), 2)
    prepare_pair(odd_row, side_a, side_b, table, ahead, extent, rhs, dense)
    prepare_pair(odd_row, side_b, side_a, table, ahead + extent, extent, rhs, dense)
    prepare(time_a, table, 0, sites, rhs, dense)
    prepare(time_b, table, sites, sites, rhs, dense)
    if not wrap_z:
        prepare(extra[0], table, ahead + 2 * extent, sites, rhs, dense)
        prepare(extra[1], table, ahead + 2 * extent + sites, sites, rhs, dense)
        extra = extra[2:]
    out_ref = extra[ITERS * 2 - 1] if last else extra[0]
    for site in range(sites):
        chosen = far_list(site, sites, depth, wrap_z, odd_time)
        slots = [table[at] for _, at in chosen]
        if dense:
            value = dense_product(slots, blocks[site, 0 : len(chosen) * out_ref.shape[-1], :])
        else:
            value = site_product(slots, [blocks[0, site, d] for d, _ in chosen])
        value = value + load_site(near_ref, site, sites, rhs, False)
        store_site(out_ref, site, sites, rhs, value, False)
    if not last:
        choose_sends(out_ref, extra[1], extra[2], extent * rhs)
    else:
        fields = list(extra[:ITERS]) + [out_ref]
        pack(rhs, fields, extra[ITERS : 2 * ITERS - 1], extra[2 * ITERS])


def pack(rhs, fields, grams, out_ref):
    period, width = grams[0].shape
    total = gram_columns(ITERS, fields, period)
    for gram in grams:
        total = total + gram[...]
    folded = total
    for turn in range(1, period // rhs):
        folded = folded + pltpu.roll(total, turn * rhs, 0)
    per_row = width // SLOT
    row = lax.broadcasted_iota(jnp.int32, (period, width), 0)
    spread = jnp.zeros((period, width), jnp.float32)
    for m in range(per_row):
        part = jnp.where(row % per_row == m, folded, 0.0)
        spread = spread + (pltpu.roll(part, SLOT * m, 1) if m else part)
    for q in range(-(-rhs // per_row)):
        summed = spread[q * per_row : q * per_row + 1]
        for m in range(1, min(per_row, rhs - q * per_row)):
            summed = summed + spread[q * per_row + m : q * per_row + m + 1]
        for copy in range(out_ref.shape[0]):
            out_ref[copy, q : q + 1, :] = summed


def tail_kernel(depth, rhs, field_ref, restriction, coarse_ref):
    restrict_field(field_ref, restriction, depth, rhs, coarse_ref, 0)


def cmulc(a, b):
    return (a[0] * b[0] + a[1] * b[1], a[0] * b[1] - a[1] * b[0])


def cmul(a, b):
    return (a[0] * b[0] - a[1] * b[1], a[0] * b[1] + a[1] * b[0])


def cadd(a, b):
    return (a[0] + b[0], a[1] + b[1])


def csub(a, b):
    return (a[0] - b[0], a[1] - b[1])


def step_coefficients(products):
    one = jnp.ones_like(products[1][0][0])

    def times(entry, value):
        if entry[1] is None:
            return (entry[0] * value[0], entry[0] * value[1])
        return cmul(entry, value)

    coeffs = [(one, jnp.zeros_like(one))]
    combined = []
    overlaps = [products[i][0] for i in range(1, ITERS + 1)]
    for step in range(ITERS):
        inner = None
        for i in range(step + 1):
            term = cmulc(coeffs[i], overlaps[i])
            inner = term if inner is None else cadd(inner, term)
        images = []
        for i in range(ITERS):
            value = None
            for j in range(step + 1):
                term = times(products[i + 1][j + 1], coeffs[j])
                value = term if value is None else cadd(value, term)
            images.append(value)
        power = None
        for i in range(step + 1):
            term = coeffs[i][0] * images[i][0] + coeffs[i][1] * images[i][1]
            power = term if power is None else power + term
        alpha = (inner[0] / power, inner[1] / power)
        overlaps = [csub(o, cmul(alpha, im)) for o, im in zip(overlaps, images)]
        scaled = [cmul(alpha, c) for c in coeffs]
        for i, value in enumerate(scaled):
            if i < len(combined):
                combined[i] = cadd(combined[i], value)
            else:
                combined.append(value)
        grown = [coeffs[0]]
        for i in range(1, step + 1):
            grown.append(csub(coeffs[i], scaled[i - 1]))
        grown.append((-scaled[step][0], -scaled[step][1]))
        coeffs = grown
    return coeffs, combined


def final_kernel(sites, rhs, groups, *refs):
    fields = refs[:ITERS]
    packed = refs[ITERS]
    coarse_refs = refs[ITERS + 1 : -7]
    sol_ref, coarse_ref, kept_ref, slice_ref, turn_ref, line_ref, rows_ref = refs[-7:]
    width = fields[0].shape[-1]
    total_rows = fields[0].shape[0]
    period = rhs
    while period % 8:
        period *= 2
    per_row = width // SLOT
    packed_rows = packed.shape[0]
    turn_ref[...] = jnp.zeros_like(turn_ref)
    turn_ref[0:packed_rows, :] = packed[...]
    turned = jnp.transpose(turn_ref[...])
    lane = lax.broadcasted_iota(jnp.int32, (SLOT, width), 1)
    quantities = jnp.zeros((SLOT, width), jnp.float32)
    for m in range(per_row):
        part = turned[SLOT * m : SLOT * m + SLOT]
        moved = pltpu.roll(part, LANES_EACH * m, 1) if m else part
        inside = (lane >= LANES_EACH * m) & (lane < LANES_EACH * m + LANES_EACH)
        quantities = jnp.where(inside, moved, quantities)

    def quantity(at):
        return jnp.broadcast_to(quantities[at : at + 1], (8, width))

    products = [[None] * (ITERS + 1) for _ in range(ITERS + 1)]
    for power in range(1, ITERS + 1):
        for other, real_lane, imag_lane in pair_slots(power):
            re = quantity(real_lane)
            im = quantity(imag_lane) if imag_lane is not None else None
            products[power][other] = (re, im)
            if other and imag_lane is not None:
                products[other][power] = (re, -im)
    coeffs, combined = step_coefficients(products)
    parts = []
    for value in coeffs[1:]:
        parts += [value[0], value[1]]
    for value in combined:
        parts += [value[0] * STEP_SCALE, value[1] * STEP_SCALE]
    line_ref[...] = jnp.zeros_like(line_ref)
    for at, part in enumerate(parts):
        line_ref[at : at + 1, :] = part[0:1]
    turn_ref[...] = jnp.transpose(line_ref[...])
    for r in range(rhs):
        j, m = divmod(r, per_row)
        source = turn_ref[LANES_EACH * m + j : LANES_EACH * m + j + 1, :]
        for at in range(r, period, rhs):
            rows_ref[at : at + 1, :] = source
    columns = rows_ref[...]
    spread = [jnp.broadcast_to(columns[:, at : at + 1], (period, width)) for at in range(len(parts))]
    sign = lane_sign(width)
    half_width = width // 2
    for base in range(0, total_rows, period):
        straight = None
        across = None
        for i in range(ITERS):
            value = fields[i][base : base + period, :]
            at = 2 * ITERS + 2 * i
            terms = (spread[at] * value, spread[at + 1] * value)
            straight = terms[0] if straight is None else straight + terms[0]
            across = terms[1] if across is None else across + terms[1]
        kept_ref[base : base + period, :] = straight - sign * pltpu.roll(across, half_width, 1)
    for site in range(sites):
        store_site(sol_ref, site, sites, rhs, load_site(kept_ref, site, sites, rhs, False), True)
    me = lax.axis_index("narrow")
    slice_rows = slice_ref.shape[0]
    cells = slice_rows // rhs
    count = len(groups)
    for k in range(len(coarse_refs) // count):
        mine = coarse_refs[k * count : (k + 1) * count]
        placed = [(ref, part) for ref, stack in zip(mine, groups) for part in range(stack)]
        for base in range(0, slice_rows, period):
            straight = None
            across = None
            for i, (ref, part) in enumerate(placed):
                row = part * slice_rows + base
                value = ref[row : row + period, :]
                if i == 0:
                    straight = value
                    continue
                terms = (spread[2 * i - 2] * value, spread[2 * i - 1] * value)
                straight = straight + terms[0]
                across = terms[1] if across is None else across + terms[1]
            slice_ref[base : base + period, :] = straight - sign * pltpu.roll(across, half_width, 1)
        target = coarse_ref.at[jnp.bitwise_xor(me, k)]
        for cell in range(cells):
            store_site(target, cell, cells, rhs, load_site(slice_ref, cell, cells, rhs, False), True)


def vmem(count):
    return [pl.BlockSpec(memory_space=pltpu.VMEM)] * count


def call(kernel, outs, *args, scratch=(), cost=None):
    single = not isinstance(outs, (list, tuple))
    return pl.pallas_call(
        kernel,
        out_shape=outs,
        in_specs=vmem(len(args)),
        out_specs=pl.BlockSpec(memory_space=pltpu.VMEM) if single else tuple(vmem(len(outs))),
        scratch_shapes=list(scratch),
        compiler_params=pltpu.CompilerParams(vmem_limit_bytes=VMEM_LIMIT),
        cost_estimate=cost,
    )(*args)


def swap_pairs(size, offset, span=None):
    span = size if span is None else span
    pairs = []
    for first in range(0, size, span):
        for i in range(offset, span + offset, 2):
            a, b = first + i % span, first + (i + 1) % span
            pairs += [(a, b), (b, a)]
    return pairs


def per_device(right_side, hop_blocks, restriction):
    sites, rhs, width = right_side.shape[1:]
    extent = sites // YLOC
    rows_y = LY // YLOC
    wide = lax.axis_size("wide")
    narrow = lax.axis_size("narrow")
    wrap_z = wide <= rows_y
    period = rhs
    while period % 8:
        period *= 2
    tile_rows = 8 * len(tile_starts(rhs))
    total_rows = sites * rhs
    half = extent * rhs
    f32 = jnp.float32
    field_shape = jax.ShapeDtypeStruct((total_rows, width), f32)
    gram_shape = jax.ShapeDtypeStruct((period, width), f32)
    far_count = max(len(far_list(site, sites, YLOC, wrap_z, 0)) for site in range(sites))
    dense_shape = jax.ShapeDtypeStruct((sites, far_count * width, width), jnp.bfloat16)
    hops = hop_blocks

    if rows_y % 2 or narrow % 2 or narrow & (narrow - 1):
        raise ValueError("odd ring")
    up_z = [(i, (i + rows_y) % wide) for i in range(wide)]
    down_z = [(b, a) for a, b in up_z]
    half_shape = jax.ShapeDtypeStruct((half, width), f32)
    block_bytes = hop_blocks.size * hop_blocks.dtype.itemsize
    field, up_send, down_send = call(
        functools.partial(open_kernel, extent),
        [field_shape, half_shape, half_shape],
        jnp.transpose(right_side[0], (1, 0, 2)),
        cost=pl.CostEstimate(flops=0, transcendentals=0, bytes_accessed=2 * block_bytes),
    )
    fields = [field]
    grams = []
    waiting = []
    sent = []
    groups = []
    cells = extent // 2
    coarse_rows = cells * rhs

    def to_all_times(value):
        arrived = [value]
        for k in range(narrow - 1, 0, -1):
            arrived.insert(1, lax.ppermute(value, "narrow", [(i, i ^ k) for i in range(narrow)]))
        return arrived

    hops = None
    table = pltpu.VMEM((sites, 4 * tile_rows, width), jnp.bfloat16)
    for power in range(ITERS):
        side_b = lax.ppermute(down_send, "wide", swap_pairs(wide, 1, rows_y))
        side_a = lax.ppermute(up_send, "wide", swap_pairs(wide, 0, rows_y))
        time_b = lax.ppermute(field, "narrow", swap_pairs(narrow, 1))
        time_a = lax.ppermute(field, "narrow", swap_pairs(narrow, 0))
        received = [side_a, side_b, time_a, time_b]
        if not wrap_z:
            received += [lax.ppermute(field, "wide", down_z), lax.ppermute(field, "wide", up_z)]
        if power == 0:
            near, hops = call(
                functools.partial(near_kernel, power, YLOC, rhs, wrap_z),
                [field_shape, jax.ShapeDtypeStruct(hop_blocks.shape, hop_blocks.dtype)],
                field,
                hop_blocks,
                scratch=[table],
            )
        elif power == 1:
            near, dense, gram = call(
                functools.partial(near_kernel, power, YLOC, rhs, wrap_z),
                [field_shape, dense_shape, gram_shape],
                *fields,
                hops,
                scratch=[table],
            )
            grams.append(gram)
        else:
            fresh = power + 1 if power == 2 else 1
            stacked = sum(ref.shape[0] for ref in waiting) + coarse_rows * fresh
            near, coarse, gram = call(
                functools.partial(near_kernel, power, YLOC, rhs, wrap_z),
                [field_shape, jax.ShapeDtypeStruct((stacked, width), f32), gram_shape],
                *fields,
                hops,
                restriction[0],
                *waiting,
                scratch=[table],
            )
            grams.append(gram)
            waiting = [coarse]
            if power >= FIRST_SEND:
                groups.append(stacked // coarse_rows)
                sent.append(to_all_times(coarse))
                waiting = []
        last = power + 1 == ITERS
        slots = 2 * sites + 2 * extent + (0 if wrap_z else 2 * sites)
        per_row = width // SLOT
        packed_rows = -(-rhs // per_row)
        outs = call(
            functools.partial(far_kernel, YLOC, rhs, wrap_z, power > 0, last),
            [field_shape]
            + (
                [jax.ShapeDtypeStruct((wide * narrow, packed_rows, width), f32)]
                if last
                else [half_shape] * 2
            ),
            near,
            dense if power else hops,
            *received,
            *(fields + grams if last else []),
            scratch=[pltpu.VMEM((slots, (2 if power else 4) * tile_rows, width), jnp.bfloat16)],
        )
        field = outs[0]
        fields.append(field)
        if not last:
            up_send, down_send = outs[1:]
        else:
            swapped = lax.all_to_all(outs[1], ("wide", "narrow"), 0, 0)
            coarse = call(
                functools.partial(tail_kernel, YLOC, rhs),
                jax.ShapeDtypeStruct((coarse_rows, width), f32),
                field,
                restriction[0],
            )
            groups.append(1)
            sent.append(to_all_times(coarse))
    totals = jnp.sum(swapped, axis=0)
    square = pltpu.VMEM((width, width), f32)
    solution_rows, slices = call(
        functools.partial(final_kernel, sites, rhs, tuple(groups)),
        [field_shape, jax.ShapeDtypeStruct((narrow, coarse_rows, width), f32)],
        *fields[:ITERS],
        totals,
        *[arrived[k] for k in range(narrow) for arrived in sent],
        scratch=[
            pltpu.VMEM((total_rows, width), f32),
            pltpu.VMEM((coarse_rows, width), f32),
            square,
            square,
            pltpu.VMEM((period, width), f32),
        ],
    )
    coarse_residual = jnp.transpose(slices.reshape(narrow, rhs, cells, width), (0, 2, 1, 3))
    solution_field = jnp.transpose(solution_rows.reshape(rhs, sites, width), (1, 0, 2))
    return solution_field[None], coarse_residual


def solution(mesh):
    placed = (
        P("narrow", "wide", None, None),
        P("narrow", "wide", None, None, None),
        P("narrow", "wide", None, None),
    )
    return jax.shard_map(
        per_device,
        mesh=mesh,
        in_specs=placed,
        out_specs=(P("narrow", "wide", None, None), P(None, "wide", None, None)),
        check_vma=False,
    )
```

```python
import functools

import jax
import jax.numpy as jnp
from jax import lax
from jax.experimental import pallas as pl
from jax.experimental.pallas import tpu as pltpu
from jax.sharding import PartitionSpec as P


ITERS = 4
YLOC = 2
LY = 16
STEP_SCALE = 0.25
FIRST_SEND = 3
LANES_EACH = 8
SLOT = 32
VMEM_LIMIT = 24 * 1024 * 1024


def tile_starts(rhs):
    starts = list(range(0, rhs - 7, 8))
    if rhs % 8:
        starts.append(rhs - 8)
    return starts


def load_site(ref, site, sites, rhs, by_rhs):
    tiles = []
    for start in tile_starts(rhs):
        if by_rhs:
            tiles.append(ref[pl.ds(start * sites + site, 8, stride=sites), :])
        else:
            tiles.append(ref[site * rhs + start : site * rhs + start + 8, :])
    return jnp.concatenate(tiles, 0)


def store_site(ref, site, sites, rhs, value, by_rhs):
    for at, start in enumerate(tile_starts(rhs)):
        tile = value[8 * at : 8 * at + 8]
        if by_rhs:
            ref[pl.ds(start * sites + site, 8, stride=sites), :] = tile
        else:
            ref[site * rhs + start : site * rhs + start + 8, :] = tile


def operand(block, sign):
    first = block * sign
    second = pltpu.roll(block, block.shape[-1] // 2, 1)
    highs = []
    lows = []
    for part in (first, second):
        high = part.astype(jnp.bfloat16)
        highs.append(high)
        lows.append((part - high.astype(jnp.float32)).astype(jnp.bfloat16))
    return jnp.concatenate(highs + lows, 0)


def split_operand(block):
    high = block.astype(jnp.bfloat16)
    low = (block - high.astype(jnp.float32)).astype(jnp.bfloat16)
    return jnp.concatenate([high, low], 0)


def lane_sign(width):
    lane = lax.broadcasted_iota(jnp.int32, (1, width), 1)
    return jnp.where(lane < width // 2, 1.0, -1.0).astype(jnp.float32)


def prepare(field_ref, table_ref, first_slot, sites, rhs, dense=False):
    sign = lane_sign(field_ref.shape[-1])
    for site in range(sites):
        block = load_site(field_ref, site, sites, rhs, False)
        table_ref[first_slot + site] = split_operand(block) if dense else operand(block, sign)


def prepare_pair(odd, even_ref, odd_ref, table_ref, first_slot, sites, rhs, dense):
    sign = lane_sign(even_ref.shape[-1])
    for site in range(sites):
        block = jnp.where(
            odd,
            load_site(odd_ref, site, sites, rhs, False),
            load_site(even_ref, site, sites, rhs, False),
        )
        table_ref[first_slot + site] = split_operand(block) if dense else operand(block, sign)


def site_product(slots, blocks):
    rows = slots[0].shape[0] // 4
    left = jnp.concatenate(slots, -1)
    right = jnp.concatenate(blocks, -1)
    total = lax.dot_general(
        left, right, (((1,), (1,)), ((), ())), preferred_element_type=jnp.float32
    )
    real_part = total[0:rows] + total[2 * rows : 3 * rows]
    imag_part = total[rows : 2 * rows] + total[3 * rows : 4 * rows]
    return jnp.concatenate([real_part, imag_part], -1) * STEP_SCALE


def columns_of(total, lanes, slot):
    summed = jnp.sum(total, axis=-1, keepdims=True)
    return jnp.where(lanes == slot, summed, 0.0)


def pair_slots(power):
    slots = []
    at = sum(2 * earlier + 1 for earlier in range(1, power))
    for other in range(power):
        slots.append((other, at, at + 1))
        at += 2
    slots.append((power, at, None))
    return slots


def gram_columns(power, refs, period):
    rows, width = refs[0].shape
    lanes = lax.broadcasted_iota(jnp.int32, (period, width), 1)
    sign = lane_sign(width)
    sums = {}
    for base in range(0, rows, period):
        mine = refs[power][base : base + period, :]
        turned = pltpu.roll(mine, width // 2, 1)
        for other, real_lane, imag_lane in pair_slots(power):
            theirs = mine if other == power else refs[other][base : base + period, :]
            for lane, factor in ((real_lane, mine), (imag_lane, turned)):
                if lane is not None:
                    term = factor * theirs
                    sums[lane] = sums[lane] + term if lane in sums else term
    out = jnp.zeros((period, width), jnp.float32)
    for _, real_lane, imag_lane in pair_slots(power):
        out = out + columns_of(sums[real_lane], lanes, real_lane)
        if imag_lane is not None:
            out = out - columns_of(sums[imag_lane] * sign, lanes, imag_lane)
    return out


def restrict_field(field_ref, restriction, depth, rhs, out_ref, base):
    width = field_ref.shape[-1]
    sign = lane_sign(width)
    extent = restriction.shape[0] // depth
    for cell in range(extent // 2):
        lefts = []
        rights = []
        for y in range(depth):
            for site in (y * extent + 2 * cell, y * extent + 2 * cell + 1):
                block = load_site(field_ref, site, 0, rhs, False)
                turned = pltpu.roll(block, width // 2, 1)
                lefts.append(jnp.concatenate([block * sign, turned], 0))
                rights.append(restriction[site])
        total = lax.dot_general(
            jnp.concatenate(lefts, -1),
            jnp.concatenate(rights, -1),
            (((1,), (1,)), ((), ())),
            precision=lax.Precision.HIGHEST,
            preferred_element_type=jnp.float32,
        )
        half = total.shape[0] // 2
        value = jnp.concatenate([total[:half], total[half:]], -1)
        for at, start in enumerate(tile_starts(rhs)):
            row = base + cell * rhs + start
            out_ref[row : row + 8, :] = value[8 * at : 8 * at + 8]


def dense_product(slots, blocks):
    total = lax.dot_general(
        jnp.concatenate(slots, -1), blocks, (((1,), (0,)), ((), ())), preferred_element_type=jnp.float32
    )
    rows = total.shape[0] // 2
    return total[:rows] + total[rows:]


def far_list(site, sites, depth, wrap_z, odd_time):
    extent = sites // depth
    ahead = 2 * sites
    behind = ahead + extent
    above = behind + extent
    below = above + sites
    y, x = divmod(site, extent)
    chosen = [(7 + odd_time, site), (8 - odd_time, sites + site)]
    if y + 1 == depth:
        chosen.append((3, ahead + x))
    if y == 0:
        chosen.append((4, behind + x))
    if not wrap_z:
        chosen += [(5, above + site), (6, below + site)]
    return chosen


def build_dense(hops_ref, dense_ref, depth, wrap_z):
    sites, _, half, width = hops_ref.shape[1:]
    odd_time = lax.rem(lax.axis_index("narrow"), 2)
    row = lax.broadcasted_iota(jnp.int32, (width, 2 * width), 0)
    col = lax.broadcasted_iota(jnp.int32, (width, 2 * width), 1)
    signed = jnp.where(row < half, STEP_SCALE, -STEP_SCALE)
    swapped = jnp.where(row < half, row + half, row - half) + width
    select = jnp.where(col == row, signed, jnp.where(col == swapped, STEP_SCALE, 0.0))
    select = select.astype(jnp.bfloat16)
    empty = jnp.zeros((half, width), jnp.bfloat16)
    for site in range(sites):
        for at, (d, _) in enumerate(far_list(site, sites, depth, wrap_z, odd_time)):
            block = hops_ref[0, site, d]
            pair = jnp.concatenate(
                [jnp.concatenate([block, empty], -1), jnp.concatenate([empty, block], -1)], 0
            )
            dense = lax.dot_general(
                select, pair, (((1,), (1,)), ((), ())), preferred_element_type=jnp.float32
            )
            dense_ref[site, at * width : (at + 1) * width, :] = dense.astype(jnp.bfloat16)


def near_sites(hops_ref, table, near_ref, depth, rhs, wrap_z, ready):
    sites = hops_ref.shape[1]
    extent = sites // depth
    for site in range(sites):
        ready(site)
        y, x = divmod(site, extent)
        chosen = [(0, site), (1, y * extent + (x + 1) % extent), (2, y * extent + (x - 1) % extent)]
        if y + 1 < depth:
            chosen.append((3, site + extent))
        if y > 0:
            chosen.append((4, site - extent))
        if wrap_z:
            chosen += [(5, site), (6, site)]
        value = site_product(
            [table[at] for _, at in chosen], [hops_ref[0, site, d] for d, _ in chosen]
        )
        store_site(near_ref, site, sites, rhs, value, False)


def open_kernel(extent, right_ref, field_ref, up_ref, down_ref):
    rhs, sites, width = right_ref.shape
    flat = right_ref.reshape(rhs * sites, width)
    for site in range(sites):
        store_site(field_ref, site, sites, rhs, load_site(flat, site, sites, rhs, True), False)
    half = extent * rhs
    choose_sends(field_ref, up_ref, down_ref, half)


def choose_sends(field_ref, up_ref, down_ref, half):
    odd = lax.rem(lax.axis_index("wide"), 2) == 1
    rows = field_ref.shape[0]
    first = field_ref[0:half, :]
    last = field_ref[rows - half : rows, :]
    up_ref[...] = jnp.where(odd, first, last)
    down_ref[...] = jnp.where(odd, last, first)


def near_kernel(power, depth, rhs, wrap_z, *refs):
    fields = refs[: power + 1]
    hops_ref = refs[power + 1]
    near_ref, other_ref, table = refs[-3:] if power == 0 else (refs[-4], refs[-2], refs[-1])
    prepare(fields[power], table, 0, hops_ref.shape[1], rhs)

    def keep(site):
        if power == 0:
            other_ref[0, site] = hops_ref[0, site]

    near_sites(hops_ref, table, near_ref, depth, rhs, wrap_z, keep)
    if power == 1:
        build_dense(hops_ref, refs[-3], depth, wrap_z)
    elif power > 1:
        restriction, coarse_ref = refs[power + 2], refs[-3]
        base = 0
        for ref in refs[power + 3 : -4]:
            coarse_ref[base : base + ref.shape[0], :] = ref[...]
            base += ref.shape[0]
        for field_ref in fields if power == 2 else fields[power:]:
            restrict_field(field_ref, restriction, depth, rhs, coarse_ref, base)
            base += restriction.shape[0] // depth // 2 * rhs
    if power:
        other_ref[...] = gram_columns(power, fields, other_ref.shape[0])


def far_kernel(depth, rhs, wrap_z, dense, last, *refs):
    near_ref, blocks, side_a, side_b, time_a, time_b = refs[:6]
    table = refs[-1]
    extra = refs[6:-1]
    extent = side_a.shape[0] // rhs
    sites = extent * depth
    ahead = 2 * sites
    odd_row = lax.rem(lax.axis_index("wide"), 2) == 1
    odd_time = lax.rem(lax.axis_index("narrow"), 2)
    prepare_pair(odd_row, side_a, side_b, table, ahead, extent, rhs, dense)
    prepare_pair(odd_row, side_b, side_a, table, ahead + extent, extent, rhs, dense)
    prepare(time_a, table, 0, sites, rhs, dense)
    prepare(time_b, table, sites, sites, rhs, dense)
    if not wrap_z:
        prepare(extra[0], table, ahead + 2 * extent, sites, rhs, dense)
        prepare(extra[1], table, ahead + 2 * extent + sites, sites, rhs, dense)
        extra = extra[2:]
    out_ref = extra[ITERS * 2 - 1] if last else extra[0]
    for site in range(sites):
        chosen = far_list(site, sites, depth, wrap_z, odd_time)
        slots = [table[at] for _, at in chosen]
        if dense:
            value = dense_product(slots, blocks[site, 0 : len(chosen) * out_ref.shape[-1], :])
        else:
            value = site_product(slots, [blocks[0, site, d] for d, _ in chosen])
        value = value + load_site(near_ref, site, sites, rhs, False)
        store_site(out_ref, site, sites, rhs, value, False)
    if not last:
        choose_sends(out_ref, extra[1], extra[2], extent * rhs)
    else:
        fields = list(extra[:ITERS]) + [out_ref]
        pack(rhs, fields, extra[ITERS : 2 * ITERS - 1], extra[2 * ITERS])


def pack(rhs, fields, grams, out_ref):
    period, width = grams[0].shape
    total = gram_columns(ITERS, fields, period)
    for gram in grams:
        total = total + gram[...]
    folded = total
    for turn in range(1, period // rhs):
        folded = folded + pltpu.roll(total, turn * rhs, 0)
    per_row = width // SLOT
    row = lax.broadcasted_iota(jnp.int32, (period, width), 0)
    spread = jnp.zeros((period, width), jnp.float32)
    for m in range(per_row):
        part = jnp.where(row % per_row == m, folded, 0.0)
        spread = spread + (pltpu.roll(part, SLOT * m, 1) if m else part)
    for q in range(-(-rhs // per_row)):
        summed = spread[q * per_row : q * per_row + 1]
        for m in range(1, min(per_row, rhs - q * per_row)):
            summed = summed + spread[q * per_row + m : q * per_row + m + 1]
        for copy in range(out_ref.shape[0]):
            out_ref[copy, q : q + 1, :] = summed


def tail_kernel(depth, rhs, field_ref, restriction, coarse_ref):
    restrict_field(field_ref, restriction, depth, rhs, coarse_ref, 0)


def cmulc(a, b):
    return (a[0] * b[0] + a[1] * b[1], a[0] * b[1] - a[1] * b[0])


def cmul(a, b):
    return (a[0] * b[0] - a[1] * b[1], a[0] * b[1] + a[1] * b[0])


def cadd(a, b):
    return (a[0] + b[0], a[1] + b[1])


def csub(a, b):
    return (a[0] - b[0], a[1] - b[1])


def step_coefficients(products):
    one = jnp.ones_like(products[1][0][0])

    def times(entry, value):
        if entry[1] is None:
            return (entry[0] * value[0], entry[0] * value[1])
        return cmul(entry, value)

    coeffs = [(one, jnp.zeros_like(one))]
    combined = []
    overlaps = [products[i][0] for i in range(1, ITERS + 1)]
    for step in range(ITERS):
        inner = None
        for i in range(step + 1):
            term = cmulc(coeffs[i], overlaps[i])
            inner = term if inner is None else cadd(inner, term)
        images = []
        for i in range(ITERS):
            value = None
            for j in range(step + 1):
                term = times(products[i + 1][j + 1], coeffs[j])
                value = term if value is None else cadd(value, term)
            images.append(value)
        power = None
        for i in range(step + 1):
            term = coeffs[i][0] * images[i][0] + coeffs[i][1] * images[i][1]
            power = term if power is None else power + term
        alpha = (inner[0] / power, inner[1] / power)
        overlaps = [csub(o, cmul(alpha, im)) for o, im in zip(overlaps, images)]
        scaled = [cmul(alpha, c) for c in coeffs]
        for i, value in enumerate(scaled):
            if i < len(combined):
                combined[i] = cadd(combined[i], value)
            else:
                combined.append(value)
        grown = [coeffs[0]]
        for i in range(1, step + 1):
            grown.append(csub(coeffs[i], scaled[i - 1]))
        grown.append((-scaled[step][0], -scaled[step][1]))
        coeffs = grown
    return coeffs, combined


def final_kernel(sites, rhs, groups, *refs):
    fields = refs[:ITERS]
    packed = refs[ITERS]
    coarse_refs = refs[ITERS + 1 : -7]
    sol_ref, coarse_ref, kept_ref, slice_ref, turn_ref, line_ref, rows_ref = refs[-7:]
    width = fields[0].shape[-1]
    total_rows = fields[0].shape[0]
    period = rhs
    while period % 8:
        period *= 2
    per_row = width // SLOT
    packed_rows = packed.shape[0]
    turn_ref[0:LANES_EACH, :] = jnp.zeros((LANES_EACH, width), jnp.float32)
    turn_ref[0:packed_rows, :] = packed[...]
    turned = jnp.transpose(turn_ref[0:LANES_EACH, :])
    line_ref[...] = jnp.zeros_like(line_ref)
    for m in range(per_row):
        line_ref[:, LANES_EACH * m : LANES_EACH * m + LANES_EACH] = turned[SLOT * m : SLOT * m + SLOT]
    quantities = line_ref[...]

    def quantity(at):
        return jnp.broadcast_to(quantities[at : at + 1], (8, width))

    products = [[None] * (ITERS + 1) for _ in range(ITERS + 1)]
    for power in range(1, ITERS + 1):
        for other, real_lane, imag_lane in pair_slots(power):
            re = quantity(real_lane)
            im = quantity(imag_lane) if imag_lane is not None else None
            products[power][other] = (re, im)
            if other and imag_lane is not None:
                products[other][power] = (re, -im)
    coeffs, combined = step_coefficients(products)
    parts = []
    for value in coeffs[1:]:
        parts += [value[0], value[1]]
    for value in combined:
        parts += [value[0] * STEP_SCALE, value[1] * STEP_SCALE]
    line_ref[...] = jnp.zeros_like(line_ref)
    for at, part in enumerate(parts):
        line_ref[at : at + 1, :] = part[0:1]
    turn_ref[:, 0:SLOT] = jnp.transpose(line_ref[...])
    for r in range(rhs):
        j, m = divmod(r, per_row)
        source = turn_ref[LANES_EACH * m + j : LANES_EACH * m + j + 1, :]
        for at in range(r, period, rhs):
            rows_ref[at : at + 1, :] = source
    columns = rows_ref[...]
    spread = [jnp.broadcast_to(columns[:, at : at + 1], (period, width)) for at in range(len(parts))]
    sign = lane_sign(width)
    half_width = width // 2
    for base in range(0, total_rows, period):
        straight = None
        across = None
        for i in range(ITERS):
            value = fields[i][base : base + period, :]
            at = 2 * ITERS + 2 * i
            terms = (spread[at] * value, spread[at + 1] * value)
            straight = terms[0] if straight is None else straight + terms[0]
            across = terms[1] if across is None else across + terms[1]
        kept_ref[base : base + period, :] = straight - sign * pltpu.roll(across, half_width, 1)
    for site in range(sites):
        store_site(sol_ref, site, sites, rhs, load_site(kept_ref, site, sites, rhs, False), True)
    me = lax.axis_index("narrow")
    slice_rows = slice_ref.shape[0]
    cells = slice_rows // rhs
    count = len(groups)
    for k in range(len(coarse_refs) // count):
        mine = coarse_refs[k * count : (k + 1) * count]
        placed = [(ref, part) for ref, stack in zip(mine, groups) for part in range(stack)]
        for base in range(0, slice_rows, period):
            straight = None
            across = None
            for i, (ref, part) in enumerate(placed):
                row = part * slice_rows + base
                value = ref[row : row + period, :]
                if i == 0:
                    straight = value
                    continue
                terms = (spread[2 * i - 2] * value, spread[2 * i - 1] * value)
                straight = straight + terms[0]
                across = terms[1] if across is None else across + terms[1]
            slice_ref[base : base + period, :] = straight - sign * pltpu.roll(across, half_width, 1)
        target = coarse_ref.at[jnp.bitwise_xor(me, k)]
        for cell in range(cells):
            store_site(target, cell, cells, rhs, load_site(slice_ref, cell, cells, rhs, False), True)


def vmem(count):
    return [pl.BlockSpec(memory_space=pltpu.VMEM)] * count


def call(kernel, outs, *args, scratch=(), cost=None):
    single = not isinstance(outs, (list, tuple))
    return pl.pallas_call(
        kernel,
        out_shape=outs,
        in_specs=vmem(len(args)),
        out_specs=pl.BlockSpec(memory_space=pltpu.VMEM) if single else tuple(vmem(len(outs))),
        scratch_shapes=list(scratch),
        compiler_params=pltpu.CompilerParams(vmem_limit_bytes=VMEM_LIMIT),
        cost_estimate=cost,
    )(*args)


def swap_pairs(size, offset, span=None):
    span = size if span is None else span
    pairs = []
    for first in range(0, size, span):
        for i in range(offset, span + offset, 2):
            a, b = first + i % span, first + (i + 1) % span
            pairs += [(a, b), (b, a)]
    return pairs


def per_device(right_side, hop_blocks, restriction):
    sites, rhs, width = right_side.shape[1:]
    extent = sites // YLOC
    rows_y = LY // YLOC
    wide = lax.axis_size("wide")
    narrow = lax.axis_size("narrow")
    wrap_z = wide <= rows_y
    period = rhs
    while period % 8:
        period *= 2
    tile_rows = 8 * len(tile_starts(rhs))
    total_rows = sites * rhs
    half = extent * rhs
    f32 = jnp.float32
    field_shape = jax.ShapeDtypeStruct((total_rows, width), f32)
    gram_shape = jax.ShapeDtypeStruct((period, width), f32)
    far_count = max(len(far_list(site, sites, YLOC, wrap_z, 0)) for site in range(sites))
    dense_shape = jax.ShapeDtypeStruct((sites, far_count * width, width), jnp.bfloat16)
    hops = hop_blocks

    if rows_y % 2 or narrow % 2 or narrow & (narrow - 1):
        raise ValueError("odd ring")
    up_z = [(i, (i + rows_y) % wide) for i in range(wide)]
    down_z = [(b, a) for a, b in up_z]
    half_shape = jax.ShapeDtypeStruct((half, width), f32)
    block_bytes = hop_blocks.size * hop_blocks.dtype.itemsize
    field, up_send, down_send = call(
        functools.partial(open_kernel, extent),
        [field_shape, half_shape, half_shape],
        jnp.transpose(right_side[0], (1, 0, 2)),
        cost=pl.CostEstimate(flops=0, transcendentals=0, bytes_accessed=2 * block_bytes),
    )
    fields = [field]
    grams = []
    waiting = []
    sent = []
    groups = []
    cells = extent // 2
    coarse_rows = cells * rhs

    def to_all_times(value):
        arrived = [value]
        for k in range(narrow - 1, 0, -1):
            arrived.insert(1, lax.ppermute(value, "narrow", [(i, i ^ k) for i in range(narrow)]))
        return arrived

    hops = None
    table = pltpu.VMEM((sites, 4 * tile_rows, width), jnp.bfloat16)
    for power in range(ITERS):
        side_b = lax.ppermute(down_send, "wide", swap_pairs(wide, 1, rows_y))
        side_a = lax.ppermute(up_send, "wide", swap_pairs(wide, 0, rows_y))
        time_b = lax.ppermute(field, "narrow", swap_pairs(narrow, 1))
        time_a = lax.ppermute(field, "narrow", swap_pairs(narrow, 0))
        received = [side_a, side_b, time_a, time_b]
        if not wrap_z:
            received += [lax.ppermute(field, "wide", down_z), lax.ppermute(field, "wide", up_z)]
        if power == 0:
            near, hops = call(
                functools.partial(near_kernel, power, YLOC, rhs, wrap_z),
                [field_shape, jax.ShapeDtypeStruct(hop_blocks.shape, hop_blocks.dtype)],
                field,
                hop_blocks,
                scratch=[table],
            )
        elif power == 1:
            near, dense, gram = call(
                functools.partial(near_kernel, power, YLOC, rhs, wrap_z),
                [field_shape, dense_shape, gram_shape],
                *fields,
                hops,
                scratch=[table],
            )
            grams.append(gram)
        else:
            fresh = power + 1 if power == 2 else 1
            stacked = sum(ref.shape[0] for ref in waiting) + coarse_rows * fresh
            near, coarse, gram = call(
                functools.partial(near_kernel, power, YLOC, rhs, wrap_z),
                [field_shape, jax.ShapeDtypeStruct((stacked, width), f32), gram_shape],
                *fields,
                hops,
                restriction[0],
                *waiting,
                scratch=[table],
            )
            grams.append(gram)
            waiting = [coarse]
            if power >= FIRST_SEND:
                groups.append(stacked // coarse_rows)
                sent.append(to_all_times(coarse))
                waiting = []
        last = power + 1 == ITERS
        slots = 2 * sites + 2 * extent + (0 if wrap_z else 2 * sites)
        per_row = width // SLOT
        packed_rows = -(-rhs // per_row)
        outs = call(
            functools.partial(far_kernel, YLOC, rhs, wrap_z, power > 0, last),
            [field_shape]
            + (
                [jax.ShapeDtypeStruct((wide * narrow, packed_rows, width), f32)]
                if last
                else [half_shape] * 2
            ),
            near,
            dense if power else hops,
            *received,
            *(fields + grams if last else []),
            scratch=[pltpu.VMEM((slots, (2 if power else 4) * tile_rows, width), jnp.bfloat16)],
        )
        field = outs[0]
        fields.append(field)
        if not last:
            up_send, down_send = outs[1:]
        else:
            swapped = lax.all_to_all(outs[1], ("narrow", "wide"), 0, 0)
            coarse = call(
                functools.partial(tail_kernel, YLOC, rhs),
                jax.ShapeDtypeStruct((coarse_rows, width), f32),
                field,
                restriction[0],
            )
            groups.append(1)
            sent.append(to_all_times(coarse))
    totals = jnp.sum(swapped, axis=0)
    solution_rows, slices = call(
        functools.partial(final_kernel, sites, rhs, tuple(groups)),
        [field_shape, jax.ShapeDtypeStruct((narrow, coarse_rows, width), f32)],
        *fields[:ITERS],
        totals,
        *[arrived[k] for k in range(narrow) for arrived in sent],
        scratch=[
            pltpu.VMEM((total_rows, width), f32),
            pltpu.VMEM((coarse_rows, width), f32),
            pltpu.VMEM((width, width), f32),
            pltpu.VMEM((SLOT, width), f32),
            pltpu.VMEM((period, width), f32),
        ],
    )
    coarse_residual = jnp.transpose(slices.reshape(narrow, rhs, cells, width), (0, 2, 1, 3))
    solution_field = jnp.transpose(solution_rows.reshape(rhs, sites, width), (1, 0, 2))
    return solution_field[None], coarse_residual


def solution(mesh):
    placed = (
        P("narrow", "wide", None, None),
        P("narrow", "wide", None, None, None),
        P("narrow", "wide", None, None),
    )
    return jax.shard_map(
        per_device,
        mesh=mesh,
        in_specs=placed,
        out_specs=(P("narrow", "wide", None, None), P(None, "wide", None, None)),
        check_vma=False,
    )
```
